32 devices in a mesh: dp: 16 (over z, y, core), tensor: 2 (over x).
Axes of the slice: x: 2, y: 2, z: 4, core: 2. Of those that a mesh axis runs over, the one named last changes fastest.
Arguments:
- hidden_in: bfloat16 [2, 16, 256, 2048], P(None, 'dp', 'tensor'), may hold values from -6 to 6
- segment_ids: int32 [2, 16, 256], P(None, 'dp'), may hold values from 0 to 1, never falling along the last dimension, each value on 1 to 192 neighbouring positions
- attn_gain: bfloat16 [2048], P('dp'), may hold values from 0.5 to 1.5
- mlp_gain: bfloat16 [2048], P('dp'), may hold values from 0.5 to 1.5
- w_query: bfloat16 [2048, 2048], P('dp', 'tensor'), may hold values from -0.125 to 0.125
- key_weight: bfloat16 [2048, 256], P('dp', 'tensor'), may hold values from -0.125 to 0.125
- value_weight: bfloat16 [2048, 256], P('dp', 'tensor'), may hold values from -0.125 to 0.125
- w_out: bfloat16 [2048, 2048], P('dp', 'tensor'), may hold values from -0.375 to 0.375
- w_gate: bfloat16 [2048, 5632], P('dp', 'tensor'), may hold values from -0.125 to 0.125
- w_up: bfloat16 [2048, 5632], P('dp', 'tensor'), may hold values from -0.125 to 0.125
- w_down: bfloat16 [2048, 5632], P('dp', 'tensor'), may hold values from -0.078125 to 0.078125
- out_cotangent: bfloat16 [2, 16, 256, 2048], P(None, 'dp', 'tensor'), may hold values from -6 to 6
Outputs:
- block_out: bfloat16 [2, 16, 256, 2048], P(None, 'dp', 'tensor')
- input_grad: float32 [2, 16, 256, 2048], P(None, 'dp', 'tensor')
- attn_gain_grad: float32 [2048], P('dp')
- mlp_gain_grad: float32 [2048], P('dp')
- w_query_grad: float32 [2048, 2048], P('dp', 'tensor')
- w_key_grad: float32 [2048, 256], P('dp', 'tensor')
- w_value_grad: float32 [2048, 256], P('dp', 'tensor')
- w_out_grad: float32 [2048, 2048], P('dp', 'tensor')
- w_gate_grad: float32 [2048, 5632], P('dp', 'tensor')
- w_up_grad: float32 [2048, 5632], P('dp', 'tensor')
- w_down_grad: float32 [2048, 5632], P('dp', 'tensor')
The draws below stay inside these ranges and needn't reach their ends.
Inputs may be any that keep to these rules, and one draw needn't show every extreme that they name: `segment_ids`: along each group's 256 tokens the ids never fall; every group holds 2 sequences, each of 64 to 192 tokens, together 256.
All inputs are finite; a program needn't handle non-finite values.
Results may differ from the reference program's by a relative error of at most 0.014.
Values may be sent and summed in bfloat16 or wider, within the bound.
No kernel may reach another device: no remote copies, remote signals or barrier semaphores. Data moves between devices by JAX's collectives and lax.ppermute only.
A program may use at most 320 MiB of HBM per device.

```python
import math
import jax
import jax.numpy as jnp
import numpy as np
from jax import lax

MODEL_WIDTH = 2048
QUERY_HEADS = 32
KEY_VALUE_HEADS = 4
HEAD_SIZE = 64
FF = 5632
MB_TOK = 256
MICRO = 2
SEGS = 2
GROUPS = 16
MOST = 192
N_DP = 16


def raised(entries, rng, source, target, blocks, factor):
    owner, partner = [(jnp.arange(entries.shape[position]) // (entries.shape[position] // blocks)).reshape([-1 if axis == position else 1 for axis in range(entries.ndim)]) for position in (source, target)]
    chosen = jax.random.permutation(rng, blocks)[partner]
    strong = (owner == chosen) | (owner == (partner + blocks // 2) % blocks)
    return jnp.where(strong, factor * entries, entries)


def block_scale(own_key, extent, shards, smallest, largest):
    loudness = 1.0
    for dim, blocks in shards:
        heights = jax.random.uniform(jax.random.fold_in(jax.random.fold_in(own_key, 6), dim), (blocks,), jnp.float32, smallest / len(shards), largest / len(shards))
        loudness = loudness * jnp.repeat(jnp.exp(heights), extent[dim] // blocks).reshape((-1,) + (1,) * (len(extent) - 1 - dim))
    return loudness


def split_up(amount, total, bound, skew):
    portions = [(1 << 20) // math.isqrt(standing ** skew) + 1 for standing in range(2, amount + 1)]
    rest, counts = total - bound - (amount - 1), [1] * (amount - 1)
    while rest > 0:
        movable = [i for i in range(amount - 1) if counts[i] < bound]
        pool, remaining = sum([portions[i] for i in movable]), rest
        for i in movable:
            extra = min(bound - counts[i], max(1, remaining * portions[i] // pool), rest)
            counts[i] = counts[i] + extra
            rest = rest - extra
    return np.array([bound] + counts)


def uneven_parts(stream_key, amount, total, most, slope):
    if amount == 2:
        one = jax.random.randint(stream_key, (), max(1, total - most), min(most, total - 1) + 1)
        return jnp.stack([one, total - one])
    lengths = jnp.asarray(split_up(amount, total, most, slope), jnp.int32)
    pairs = (amount - 1) // 2
    donor, taker = lengths[1:1 + 2 * pairs:2], lengths[2:2 + 2 * pairs:2]
    room = jnp.minimum(donor - 1, most - taker)
    passed = jax.random.randint(jax.random.fold_in(stream_key, 1), (pairs,), 0, 1 << 20) % (room + 1)
    lengths = lengths.at[1:1 + 2 * pairs:2].set(donor - passed).at[2:2 + 2 * pairs:2].set(taker + passed)
    return lengths[jax.random.permutation(jax.random.fold_in(stream_key, 2), amount)]


def scatter_about(own_key, extent, width, limit, cuts=(), kind=jnp.bfloat16):
    values = width * jax.random.normal(own_key, extent, jnp.float32)
    if cuts:
        values = values * block_scale(own_key, extent, cuts, -0.22, 0.18)
    return jnp.clip(values, -limit, limit).astype(kind)


def heavy_noise(rng, shape, spread, limit, shards, heavy, held_as=jnp.bfloat16):
    array = spread * jax.random.normal(rng, shape, jnp.float32)
    if shards:
        array = array * block_scale(rng, shape, shards, -0.22, 0.18)
    return jnp.clip(raised(array, jax.random.fold_in(rng, 3), *heavy), -limit, limit).astype(held_as)


def setup_inputs(seed: int = 0) -> dict:
    seeds = jax.random.split(jax.random.key(seed), 13)
    return {
        "hidden_in": heavy_noise(seeds[0], (MICRO, GROUPS, MB_TOK, MODEL_WIDTH), 1.0, 6.0, ((1, 16), (2, 2)), (1, 3, 16, 2.0)),
        "segment_ids": jax.vmap(lambda own: jnp.searchsorted(jnp.cumsum(uneven_parts(own, SEGS, MB_TOK, MOST, 2)), jnp.arange(MB_TOK), side="right"))(jax.random.split(seeds[1], MICRO * GROUPS)).reshape((MICRO, GROUPS, MB_TOK)).astype(jnp.int32),
        "attn_gain": jnp.clip(1.0 + 0.1 * jax.random.normal(seeds[2], (MODEL_WIDTH,), jnp.float32), 0.5, 1.5).astype(jnp.bfloat16),
        "mlp_gain": jnp.clip(1.0 + 0.1 * jax.random.normal(seeds[3], (MODEL_WIDTH,), jnp.float32), 0.5, 1.5).astype(jnp.bfloat16),
        "w_query": scatter_about(seeds[4], (MODEL_WIDTH, QUERY_HEADS * HEAD_SIZE), MODEL_WIDTH ** -0.5, 0.125, ((0, 16), (1, 2))),
        "key_weight": scatter_about(seeds[5], (MODEL_WIDTH, KEY_VALUE_HEADS * HEAD_SIZE), MODEL_WIDTH ** -0.5, 0.125, ((0, 16), (1, 2))),
        "value_weight": scatter_about(seeds[6], (MODEL_WIDTH, KEY_VALUE_HEADS * HEAD_SIZE), MODEL_WIDTH ** -0.5, 0.125, ((0, 16), (1, 2))),
        "w_out": scatter_about(seeds[7], (MODEL_WIDTH, QUERY_HEADS * HEAD_SIZE), (QUERY_HEADS * HEAD_SIZE // 8) ** -0.5, 0.375, ((0, 16), (1, 2))),
        "w_gate": scatter_about(seeds[8], (MODEL_WIDTH, FF), MODEL_WIDTH ** -0.5, 0.125, ((0, 16), (1, 2))),
        "w_up": scatter_about(seeds[9], (MODEL_WIDTH, FF), MODEL_WIDTH ** -0.5, 0.125, ((0, 16), (1, 2))),
        "w_down": scatter_about(seeds[10], (MODEL_WIDTH, FF), FF ** -0.5, 0.078125, ((0, 16), (1, 2))),
        "out_cotangent": heavy_noise(seeds[11], (MICRO, GROUPS, MB_TOK, MODEL_WIDTH), 1.0, 6.0, ((1, 16), (2, 2)), (1, 3, 16, 2.0)),
    }


@jax.custom_vjp
def lower_half(v):
    return lax.optimization_barrier(v.astype(jnp.bfloat16)).astype(jnp.float32)

@jax.custom_vjp
def lower_half_back(v):
    return v

def low_keep(v):
    return (lower_half(v), None)

def low_pass(kept, grad):
    return (grad,)

def back_keep(v):
    return (v, None)

def back_low(kept, grad):
    return (lower_half(grad),)
lower_half.defvjp(low_keep, low_pass)
lower_half_back.defvjp(back_keep, back_low)
norm_eps = 1e-05

def rotary_tables(segment_row, head_dim):
    length_total = segment_row.shape[0]
    same_seq = segment_row[:, None] == segment_row[None, :]
    row_ids = lax.broadcasted_iota(jnp.int32, (length_total, length_total), 0)
    col_ids = lax.broadcasted_iota(jnp.int32, (length_total, length_total), 1)
    earlier = jnp.logical_and(same_seq, col_ids < row_ids)
    places = lax.optimization_barrier(jnp.sum(earlier.astype(jnp.float32), axis=1))
    allowed = jnp.logical_and(same_seq, col_ids <= row_ids)
    freq_index = jnp.arange(head_dim // 2, dtype=jnp.float32)
    inverse = 10000.0 ** (-2.0 * freq_index / head_dim)
    angles = places[:, None] * inverse[None, :]
    cosine_table = jnp.concatenate([jnp.cos(angles), jnp.cos(angles)], axis=1)
    sine_table = jnp.concatenate([jnp.sin(angles), jnp.sin(angles)], axis=1)
    return (allowed, cosine_table, sine_table)

def rotate_pairs(values_in, cosine_table, sine_table):
    half_width = values_in.shape[-1] // 2
    turned = jnp.concatenate([-values_in[..., half_width:], values_in[..., :half_width]], axis=-1)
    return values_in * cosine_table[:, None, :] + turned * sine_table[:, None, :]

def layer(row_block, gain_a, gain_m, w_query, key_weight, value_weight, w_out, w_gate, w_up, w_down, allowed, cosine_table, sine_table):
    highest = lax.Precision.HIGHEST
    length_total = row_block.shape[0]
    group_length = QUERY_HEADS // KEY_VALUE_HEADS
    score_scale = HEAD_SIZE ** (-0.5)

    def product_result(left, right):
        return jnp.dot(left, right, precision=highest, preferred_element_type=jnp.float32)
    scale_a = lax.rsqrt(lax.optimization_barrier(jnp.mean(row_block * row_block, axis=-1, keepdims=True)) + norm_eps)
    attention_normed = lower_half(row_block * scale_a * gain_a)
    query_linear = lower_half_back(product_result(attention_normed, w_query)).reshape(length_total, QUERY_HEADS, HEAD_SIZE)
    key_linear = lower_half_back(product_result(attention_normed, key_weight)).reshape(length_total, KEY_VALUE_HEADS, HEAD_SIZE)
    value_rows = lower_half(lower_half_back(product_result(attention_normed, value_weight))).reshape(length_total, KEY_VALUE_HEADS, HEAD_SIZE)
    query_rows = lower_half(rotate_pairs(query_linear, cosine_table, sine_table)).reshape(length_total, KEY_VALUE_HEADS, group_length, HEAD_SIZE)
    keys = lower_half(rotate_pairs(key_linear, cosine_table, sine_table))
    scores = lower_half_back(jnp.einsum('qkgd,skd->kgqs', query_rows, keys, precision=highest) * score_scale)
    scores = jnp.where(allowed[None, None], scores, -1e+30)
    probs = jax.nn.softmax(scores, axis=-1)
    attended = jnp.einsum('kgqs,skd->qkgd', lower_half(probs), value_rows, precision=highest).reshape(length_total, QUERY_HEADS * HEAD_SIZE)
    attended = lower_half(lower_half_back(attended))
    attn_out = lower_half_back(product_result(attended, w_out.T))
    mid = row_block + attn_out
    scale_m = lax.rsqrt(lax.optimization_barrier(jnp.mean(mid * mid, axis=-1, keepdims=True)) + norm_eps)
    normed_m = lower_half(mid * scale_m * gain_m)
    gate_lin = lower_half_back(product_result(normed_m, w_gate))
    up_lin = lower_half_back(product_result(normed_m, w_up))
    inner_act = lower_half(jax.nn.silu(gate_lin) * up_lin)
    mlp_out = lower_half_back(product_result(inner_act, w_down.T))
    return mid + mlp_out

def reference(hidden_in, segment_ids, attn_gain, mlp_gain, w_query, key_weight, value_weight, w_out, w_gate, w_up, w_down, out_cotangent):
    weights = tuple((weight.astype(jnp.float32) for weight in (attn_gain, mlp_gain, w_query, key_weight, value_weight, w_out, w_gate, w_up, w_down)))
    row_all = hidden_in.astype(jnp.float32).reshape(MICRO * N_DP, MB_TOK, MODEL_WIDTH)
    cot_all = out_cotangent.astype(jnp.float32).reshape(MICRO * N_DP, MB_TOK, MODEL_WIDTH)
    seg_all = segment_ids.reshape(MICRO * N_DP, MB_TOK)

    def group_step(totals, item):
        row_block, segment_row, cot_rows = item
        allowed, cosine_table, sine_table = rotary_tables(segment_row, HEAD_SIZE)

        def forward(rows_in, *weight_list):
            return layer(rows_in, *weight_list, allowed, cosine_table, sine_table)
        result, pull_back = jax.vjp(forward, row_block, *weights)
        grads = pull_back(cot_rows)
        totals = tuple((left_sum + right_sum for left_sum, right_sum in zip(totals, grads[1:])))
        return (totals, (result.astype(jnp.bfloat16), grads[0]))
    zero_grads = tuple((jnp.zeros(weight.shape, jnp.float32) for weight in weights))
    totals, (block_rows, input_grads) = lax.scan(group_step, zero_grads, (row_all, seg_all, cot_all))
    block_out = block_rows.reshape(MICRO, N_DP, MB_TOK, MODEL_WIDTH)
    input_grad = input_grads.reshape(MICRO, N_DP, MB_TOK, MODEL_WIDTH)
    return (block_out, input_grad, totals[0], totals[1], totals[2], totals[3], totals[4], totals[5], totals[6], totals[7], totals[8])
```

```python
import jax
import jax.numpy as jnp
from jax import lax
from jax.sharding import Mesh
from jax.sharding import PartitionSpec as P

HEAD_SIZE = 64
EPS = 1e-05
BF = jnp.bfloat16
F32 = jnp.float32


def swap_x(a):
    return lax.ppermute(a, "x", [(0, 1), (1, 0)])


def swap_y(a):
    return lax.ppermute(a, "y", [(0, 1), (1, 0)])


def swap_c(a):
    return lax.ppermute(a, "c", [(0, 1), (1, 0)])


def swap_z(a, bit):
    n = lax.axis_size("z")
    return lax.ppermute(a, "z", [(i, i ^ bit) for i in range(n)])


def far_bits():
    n = lax.axis_size("z")
    bits = []
    bit = n // 2
    while bit:
        bits.append(bit)
        bit //= 2
    return bits


def z_order():
    order = [0]
    for bit in far_bits():
        order = order + [r ^ bit for r in order]
    return order


def gather_tokens(own):
    half = own.shape[-1] // 2
    from_x = swap_x(own)
    from_y = swap_y(own)
    diag_low = swap_y(from_x[..., :half])
    diag_high = swap_x(from_y[..., half:])
    diag = jnp.concatenate([diag_low, diag_high], axis=-1)
    return jnp.concatenate([own, from_x, from_y, diag], axis=1)


def scatter_tokens(part):
    m, rows, f = part.shape
    half = f // 2
    part = part.reshape(m, 4, rows // 4, f)
    diag = part[:, 3]
    low = swap_y(diag[..., :half])
    high = swap_x(diag[..., half:])
    to_x = part[:, 1]
    to_y = part[:, 2]
    to_x = jnp.concatenate(
        [(to_x[..., :half].astype(F32) + low.astype(F32)).astype(BF), to_x[..., half:]], axis=-1
    )
    to_y = jnp.concatenate(
        [to_y[..., :half], (to_y[..., half:].astype(F32) + high.astype(F32)).astype(BF)], axis=-1
    )
    from_x = swap_x(to_x)
    from_y = swap_y(to_y)
    return part[:, 0].astype(F32) + from_x.astype(F32) + from_y.astype(F32)


def column_part(a, index):
    width = a.shape[1] // 2
    return lax.dynamic_slice_in_dim(a, index * width, width, axis=1)


def gather_rows(mine, from_y, y):
    first = y == 0
    own = jnp.concatenate([jnp.where(first, mine, from_y), jnp.where(first, from_y, mine)], axis=0)
    pieces = [own]
    for bit in far_bits():
        pieces = pieces + [swap_z(p, bit) for p in pieces]
    return pieces + [swap_c(p) for p in pieces]


def reduce_rows(grad):
    half = grad.shape[0] // 2
    got = swap_c(grad[half:])
    grad = grad[:half].astype(F32) + got.astype(F32)
    for bit in reversed(far_bits()):
        half = grad.shape[0] // 2
        got = swap_z(grad[half:].astype(BF), bit)
        grad = grad[:half] + got.astype(F32)
    return grad


def finish_rows(grad, y):
    block = grad.shape[0] // 2
    mine = lax.dynamic_slice_in_dim(grad, y * block, block, axis=0)
    send = lax.dynamic_slice_in_dim(grad, (1 - y) * block, block, axis=0)
    return mine, swap_y(send.astype(BF)).astype(F32)


def join(mine, got, y):
    first = y == 0
    return jnp.concatenate([jnp.where(first, mine, got), jnp.where(first, got, mine)], axis=1)


def rows_rows(left, right):
    return lax.dot_general(left, right, (((0,), (0,)), ((), ())), preferred_element_type=F32)


def cols_cols(left, right):
    return lax.dot_general(left, right, (((1,), (1,)), ((), ())), preferred_element_type=F32)


def rotate(v, cos, sin):
    half = v.shape[-1] // 2
    turned = jnp.concatenate([-v[..., half:], v[..., :half]], axis=-1)
    return v * cos + turned * sin


def rotate_back(v, cos, sin):
    half = v.shape[-1] // 2
    w = v * sin
    turned = jnp.concatenate([w[..., half:], -w[..., :half]], axis=-1)
    return v * cos + turned


def norm_back(d_normed, unit, gain, scale):
    d_unit = d_normed * gain
    return scale * (d_unit - unit * jnp.mean(d_unit * unit, axis=-1, keepdims=True))


def on_device(
    hidden_in,
    segment_ids,
    attn_gain,
    mlp_gain,
    w_query,
    key_weight,
    value_weight,
    w_out,
    w_gate,
    w_up,
    w_down,
    out_cotangent,
):
    z, y, c, x = (lax.axis_index(n) for n in ("z", "y", "c", "x"))
    nz = lax.axis_size("z")
    micro = hidden_in.shape[0]
    toks = hidden_in.shape[2]
    width = hidden_in.shape[3]
    block = w_query.shape[0]
    scale = HEAD_SIZE ** (-0.5)
    order = z_order()
    spots = [
        (((z ^ rz) * 2 + yy) * 2 + (c ^ rc)) for rc in range(2) for rz in order for yy in range(2)
    ]

    def to_rel(a):
        return jnp.concatenate(
            [lax.dynamic_slice_in_dim(a, s * block, block, axis=a.ndim - 1) for s in spots], axis=-1
        )

    where_c = [z * 0 + (cc ^ c) for cc in range(2)]
    rank = jnp.array([order.index(r) for r in range(nz)], jnp.int32)

    def from_rel(a):
        parts = []
        for zz in range(nz):
            for yy in range(2):
                for cc in range(2):
                    spot = ((where_c[cc] * nz) + rank[z ^ zz]) * 2 + yy
                    parts.append(
                        lax.dynamic_slice_in_dim(a, spot * block, block, axis=a.ndim - 1)
                    )
        return jnp.concatenate(parts, axis=-1)

    def pack_attn(index):
        pads = jnp.zeros((16 - 2, block), BF)
        gains = jnp.concatenate([attn_gain[None], mlp_gain[None], pads], axis=0)
        body = jnp.concatenate(
            [
                column_part(w_query, index),
                column_part(key_weight, index),
                column_part(value_weight, index),
                column_part(w_out, index),
            ],
            axis=1,
        )
        gains = jnp.pad(gains, ((0, 0), (0, body.shape[1] - block)))
        return jnp.concatenate([body, gains], axis=0)

    hid = to_rel(hidden_in[:, 0])
    hid_all = gather_tokens(hid)
    other_ids = swap_y(segment_ids[:, 0])

    attn_pieces = gather_rows(pack_attn(y), swap_y(pack_attn(1 - y)), y)
    gu_mine = jnp.concatenate([column_part(w_gate, y), column_part(w_up, y)], axis=1)
    gu_send = jnp.concatenate([column_part(w_gate, 1 - y), column_part(w_up, 1 - y)], axis=1)
    gu_pieces = gather_rows(gu_mine, swap_y(gu_send), y)
    down_pieces = gather_rows(column_part(w_down, y), swap_y(column_part(w_down, 1 - y)), y)

    tall = block + 16
    body = [p[s * tall : s * tall + block] for p in attn_pieces for s in range(2)]
    attn_w = jnp.concatenate(body, axis=0)
    gains = jnp.concatenate(
        [p[s * tall + block : s * tall + block + 2, :block] for p in attn_pieces for s in range(2)],
        axis=1,
    ).astype(F32)
    gain_a, gain_m = gains[0], gains[1]
    q_cols = w_query.shape[1] // 2
    kv_cols = key_weight.shape[1] // 2
    qkv_cols = q_cols + 2 * kv_cols
    qkv_w = attn_w[:, :qkv_cols]
    out_w = attn_w[:, qkv_cols:]
    gu_w = jnp.concatenate(gu_pieces, axis=0)
    down_w = jnp.concatenate(down_pieces, axis=0)
    cot = to_rel(out_cotangent[:, 0])
    cot_all = gather_tokens(cot)

    length = 2 * toks
    groups = micro * 2
    ids = jnp.stack([segment_ids[:, 0], other_ids], axis=1).reshape(groups, length)
    ids = jnp.where(x == 0, ids, jnp.roll(ids, toks, axis=1))
    pos = (jnp.arange(length, dtype=jnp.int32) + toks * x) % length
    same = ids[:, :, None] == ids[:, None, :]
    allowed = jnp.logical_and(same, (pos[None, :] <= pos[:, None])[None])
    places = jnp.sum(allowed.astype(F32), axis=2) - 1.0
    freq = jnp.arange(HEAD_SIZE // 2, dtype=F32)
    inverse = 10000.0 ** (-2.0 * freq / HEAD_SIZE)
    angles = places[:, :, None] * inverse
    cos = jnp.concatenate([jnp.cos(angles)] * 2, axis=-1)
    sin = jnp.concatenate([jnp.sin(angles)] * 2, axis=-1)

    rows = micro * 4 * toks
    hid32 = hid_all.astype(F32).reshape(rows, width)
    scale_a = lax.rsqrt(jnp.mean(hid32 * hid32, axis=-1, keepdims=True) + EPS)
    unit_a_all = hid32 * scale_a
    normed_a = (unit_a_all * gain_a).astype(BF)
    qkv = jnp.dot(normed_a, qkv_w, preferred_element_type=F32)
    heads = q_cols // HEAD_SIZE
    q_lin = qkv[:, :q_cols].reshape(groups, length, heads, HEAD_SIZE)
    k_lin = qkv[:, q_cols : q_cols + kv_cols].reshape(groups, length, HEAD_SIZE)
    values = qkv[:, q_cols + kv_cols :].astype(BF).reshape(groups, length, HEAD_SIZE)
    queries = rotate(q_lin, cos[:, :, None], sin[:, :, None]).astype(BF)
    keys = rotate(k_lin, cos, sin).astype(BF)
    scores = jnp.einsum("gqhd,gsd->ghqs", queries, keys, preferred_element_type=F32) * scale
    scores = jnp.where(allowed[:, None], scores, -1e30)
    top = jnp.max(scores, axis=-1, keepdims=True)
    expo = jnp.exp(scores - top)
    probs = expo / jnp.sum(expo, axis=-1, keepdims=True)
    attended = jnp.einsum("ghqs,gsd->gqhd", probs.astype(BF), values, preferred_element_type=F32)
    attended = attended.reshape(rows, q_cols).astype(BF)
    attn_part = cols_cols(attended, out_w).astype(BF).reshape(micro, 4 * toks, width)
    mid = hid.astype(F32) + scatter_tokens(attn_part)

    scale_m = lax.rsqrt(jnp.mean(mid * mid, axis=-1, keepdims=True) + EPS)
    unit_m = mid * scale_m
    normed_m = gather_tokens((unit_m * gain_m).astype(BF)).reshape(rows, width)
    gu = jnp.dot(normed_m, gu_w, preferred_element_type=F32)
    ff = gu.shape[1] // 2
    gate, up = gu[:, :ff], gu[:, ff:]
    sig = jax.nn.sigmoid(gate)
    silu = gate * sig
    inner = (silu * up).astype(BF)
    cot_rows = cot_all.reshape(rows, width)
    g_down = rows_rows(cot_rows, inner).astype(BF)
    g_down = reduce_rows(g_down)
    d_inner = jnp.dot(cot_rows, down_w, preferred_element_type=F32)
    d_gate = (d_inner * up * sig * (1.0 + gate * (1.0 - sig))).astype(BF)
    d_up = (d_inner * silu).astype(BF)
    d_gu = jnp.concatenate([d_gate, d_up], axis=1)
    back_mlp = cols_cols(d_gu, gu_w).astype(BF).reshape(micro, 4 * toks, width)
    d_normed_m = scatter_tokens(back_mlp)
    g_gu = reduce_rows(rows_rows(normed_m, d_gu).astype(BF))
    mlp_part = cols_cols(inner, down_w).astype(BF).reshape(micro, 4 * toks, width)
    block_out = (mid + scatter_tokens(mlp_part)).astype(BF)
    gain_m_part = jnp.sum(d_normed_m * unit_m, axis=(0, 1))
    d_mid = cot.astype(F32) + norm_back(d_normed_m, unit_m, gain_m, scale_m)

    d_mid_all = gather_tokens(d_mid.astype(BF)).reshape(rows, width)
    d_att = jnp.dot(d_mid_all, out_w, preferred_element_type=F32).astype(BF)
    g_out = rows_rows(d_mid_all, attended).astype(BF)
    d_att = d_att.reshape(groups, length, heads, HEAD_SIZE)
    d_probs = jnp.einsum("gqhd,gsd->ghqs", d_att, values, preferred_element_type=F32)
    inner_sum = jnp.sum(probs * d_probs, axis=-1, keepdims=True)
    d_scores = (probs * (d_probs - inner_sum)).astype(BF)
    d_queries = jnp.einsum("ghqs,gsd->gqhd", d_scores, keys, preferred_element_type=F32) * scale
    d_keys = jnp.einsum("ghqs,gqhd->gsd", d_scores, queries, preferred_element_type=F32) * scale
    d_values = jnp.einsum("ghqs,gqhd->gsd", probs.astype(BF), d_att, preferred_element_type=F32)
    d_q = rotate_back(d_queries, cos[:, :, None], sin[:, :, None]).reshape(rows, q_cols)
    d_k = rotate_back(d_keys, cos, sin).reshape(rows, kv_cols)
    d_v = d_values.reshape(rows, kv_cols)
    d_qkv = jnp.concatenate([d_q, d_k, d_v], axis=1).astype(BF)
    back_attn = cols_cols(d_qkv, qkv_w)
    gain_a_part = jnp.sum(back_attn * unit_a_all, axis=0)
    g_qkv = rows_rows(normed_a, d_qkv).astype(BF)

    g_out = reduce_rows(g_out)
    g_qkv = reduce_rows(g_qkv)
    d_normed_a = scatter_tokens(back_attn.astype(BF).reshape(micro, 4 * toks, width))
    unit_a = unit_a_all.reshape(micro, 4 * toks, width)[:, :toks]
    sc_a = scale_a.reshape(micro, 4 * toks, 1)[:, :toks]
    input_grad = d_mid + norm_back(d_normed_a, unit_a, gain_a, sc_a)

    gain_parts = jnp.stack([gain_a_part, gain_m_part]).reshape(2, 2 * nz, 2 * block)
    gain_parts = gain_parts.transpose(1, 0, 2).reshape(2 * nz * 2, 2 * block)
    half = gain_parts.shape[0] // 2
    gsum = gain_parts[:half] + swap_c(gain_parts[half:])
    for bit in reversed(far_bits()):
        half = gsum.shape[0] // 2
        gsum = gsum[:half] + swap_z(gsum[half:], bit)
    gsum = gsum.reshape(2, 2, block)
    keep = lax.dynamic_slice_in_dim(gsum, y, 1, axis=1)[:, 0]
    give = lax.dynamic_slice_in_dim(gsum, 1 - y, 1, axis=1)[:, 0]
    keep = keep + swap_y(give)
    keep = keep + swap_x(keep)

    down_m, down_r = finish_rows(g_down, y)
    gu_m, gu_r = finish_rows(g_gu, y)
    out_m, out_r = finish_rows(g_out, y)
    qkv_m, qkv_r = finish_rows(g_qkv, y)

    def cut(lo, hi):
        return join(qkv_m[:, lo:hi], qkv_r[:, lo:hi], y)

    return (
        from_rel(block_out)[:, None],
        from_rel(input_grad)[:, None],
        keep[0],
        keep[1],
        cut(0, q_cols),
        cut(q_cols, q_cols + kv_cols),
        cut(q_cols + kv_cols, qkv_cols),
        join(out_m, out_r, y),
        join(gu_m[:, :ff], gu_r[:, :ff], y),
        join(gu_m[:, ff:], gu_r[:, ff:], y),
        join(down_m, down_r, y),
    )


def solution(mesh):
    n_dp, n_tensor = mesh.shape["dp"], mesh.shape["tensor"]
    grid = Mesh(mesh.devices.reshape(n_dp // 4, 2, 2, n_tensor), ("z", "y", "c", "x"))
    dp = ("z", "y", "c")
    token = P(None, dp, "x", None)
    weight = P(dp, "x")
    gain = P(dp)
    in_specs = (token, P(None, dp, None), gain, gain) + (weight,) * 7 + (token,)
    out_specs = (token, token, gain, gain) + (weight,) * 7
    return jax.shard_map(
        on_device, mesh=grid, in_specs=in_specs, out_specs=out_specs, check_vma=False
    )
```

```python
import jax
import jax.numpy as jnp
import numpy as np
from jax import lax
from jax.experimental import pallas as pl
from jax.experimental.pallas import tpu as pltpu
from jax.sharding import Mesh
from jax.sharding import PartitionSpec as P

HEAD_SIZE = 64
EPS = 1e-05
BF = jnp.bfloat16
F32 = jnp.float32


def swap_x(a):
    return lax.ppermute(a, "x", [(0, 1), (1, 0)])


def swap_y(a):
    return lax.ppermute(a, "y", [(0, 1), (1, 0)])


def swap_c(a):
    return lax.ppermute(a, "c", [(0, 1), (1, 0)])


def swap_z(a, bit):
    n = lax.axis_size("z")
    return lax.ppermute(a, "z", [(i, i ^ bit) for i in range(n)])


def far_bits():
    n = lax.axis_size("z")
    bits = []
    bit = n // 2
    while bit:
        bits.append(bit)
        bit //= 2
    return bits


def z_order():
    order = [0]
    for bit in far_bits():
        order = order + [r ^ bit for r in order]
    return order


def meet(*values):
    return lax.optimization_barrier(values)


def single(work, *args):
    shapes = jax.eval_shape(work, *args)
    return lax.cond(
        lax.axis_index("z") >= 0,
        work,
        lambda *_: jax.tree.map(lambda s: jnp.zeros(s.shape, s.dtype), shapes),
        *args,
    )


def gather_near(own):
    return own, swap_x(own), swap_y(own)


def gather_diag(near):
    _, from_x, from_y = near
    half = from_x.shape[-1] // 2
    return swap_y(from_x[..., :half]), swap_x(from_y[..., half:])


def gather_join(near, diag):
    return jnp.concatenate(tuple(near) + (jnp.concatenate(diag, axis=-1),), axis=1)


def gather_far(near):
    return gather_join(near, gather_diag(near))


def scatter_far(part):
    m, rows, f = part.shape
    diag = part[:, 3 * rows // 4 :]
    return swap_y(diag[..., : f // 2]), swap_x(diag[..., f // 2 :])


def scatter_prep(part, far):
    m, rows, f = part.shape
    half = f // 2
    low, high = far
    part = part.reshape(m, 4, rows // 4, f)
    to_x = part[:, 1]
    to_y = part[:, 2]
    to_x = jnp.concatenate(
        [(to_x[..., :half].astype(F32) + low.astype(F32)).astype(BF), to_x[..., half:]], axis=-1
    )
    to_y = jnp.concatenate(
        [to_y[..., :half], (to_y[..., half:].astype(F32) + high.astype(F32)).astype(BF)], axis=-1
    )
    return to_x, to_y


def scatter_near(to_x, to_y):
    return swap_x(to_x), swap_y(to_y)


def scatter_sum(part, near):
    rows = part.shape[1] // 4
    return part[:, :rows].astype(F32) + near[0].astype(F32) + near[1].astype(F32)


def column_part(a, index):
    width = a.shape[1] // 2
    return lax.dynamic_slice_in_dim(a, index * width, width, axis=1)


def pick(a, axis, index):
    return lax.dynamic_index_in_dim(a, index, axis, keepdims=False)


def z_first(*shards):
    held = jnp.stack(shards)[None]
    return held, swap_z(held, far_bits()[0])


def z_rest(pair):
    held = jnp.concatenate(pair, axis=0)
    bits = far_bits()[1:]
    for bit in bits[:-1]:
        held = jnp.concatenate([held, swap_z(held, bit)], axis=0)
    return held, swap_z(held, bits[-1])


def both(pair):
    return jnp.concatenate(pair, axis=0)


def assemble(streams, z, y, extra=0, split=()):
    order = np.array(z_order() + [0], np.int32)
    n, rows, cols = streams[0].shape
    block = rows - extra
    last = np.arange(n + 1) == n
    where = jnp.where(jnp.asarray(last), y, jnp.asarray(order) ^ z)

    edges = (0,) + tuple(split) + (cols,)
    spans = list(zip(edges[:-1], edges[1:]))

    def kernel(where_ref, own, own_c, peer, peer_c, *more):
        yy = where_ref[n]
        for ref, at_c, at_y in ((own, 0, yy), (own_c, 1, yy), (peer, 0, 1 - yy), (peer_c, 1, 1 - yy)):
            if not extra:
                more[0][at_c, 0, at_y] = ref[0]
                continue
            for out, (lo, hi) in zip(more, spans):
                out[at_c, 0, at_y] = ref[0, :block, lo:hi]
            more[-1][at_c, 0, at_y] = ref[0, block:, :128]

    out_shape = [jax.ShapeDtypeStruct((2, n, 2, block, hi - lo), BF) for lo, hi in spans]
    out_specs = [
        pl.BlockSpec((2, 1, 2, block, hi - lo), lambda i, at: (0, at[i], 0, 0, 0)) for lo, hi in spans
    ]
    if extra:
        out_shape.append(jax.ShapeDtypeStruct((2, n, 2, extra, 128), BF))
        out_specs.append(pl.BlockSpec((2, 1, 2, extra, 128), lambda i, at: (0, at[i], 0, 0, 0)))
    moved = 4 * n * rows * cols * 4
    return pl.pallas_call(
        kernel,
        out_shape=out_shape,
        grid_spec=pltpu.PrefetchScalarGridSpec(
            num_scalar_prefetch=1,
            grid=(n,),
            in_specs=[pl.BlockSpec((1, rows, cols), lambda i, at: (i, 0, 0))] * 4,
            out_specs=out_specs,
        ),
        cost_estimate=pl.CostEstimate(flops=0, bytes_accessed=moved, transcendentals=0),
    )(where, *streams)


def grad_half(index, left, right):
    nz = lax.axis_size("z")
    half = left.shape[1] // 2
    part = rows_rows(left[:, index * half : (index + 1) * half], right).astype(BF)
    return part.reshape(nz, 2, half // (2 * nz), right.shape[1])


def add(a, b):
    return a.astype(F32) + b.astype(F32)


def reduce_step(grad, z, bit):
    n, _, block, cols = grad.shape
    pairs = grad.reshape(n // 2, 2, 2, block, cols)
    here = (z // bit) % 2
    return pick(pairs, 1, here), swap_z(pick(pairs, 1, 1 - here).astype(BF), bit)


def reduce_near(pair, z):
    return reduce_step(add(*pair), z, 1)


def reduce_far(pair, z):
    grad = add(*pair)
    bits = far_bits()[:-1][::-1]
    for bit in bits[:-1]:
        grad = add(*reduce_step(grad, z, bit))
    return reduce_step(grad, z, bits[-1])


def reduce_y(pair, y):
    grad = add(*pair)[0]
    return pick(grad, 0, y), swap_y(pick(grad, 0, 1 - y).astype(BF)).astype(F32)


def join(parts, y):
    mine, got = parts
    first = y == 0
    return jnp.concatenate([jnp.where(first, mine, got), jnp.where(first, got, mine)], axis=1)


def regroup(a, block, c, back=False):
    m, rows, width = a.shape
    half = width // 2
    count = half // block
    if block % 128:
        first = c == 0
        if back:
            own, other = (p.reshape(m, rows, count, block) for p in (a[..., :half], a[..., half:]))
            pair = jnp.stack([jnp.where(first, own, other), jnp.where(first, other, own)], axis=3)
            return pair.reshape(m, rows, width)
        pair = a.reshape(m, rows, count, 2, block)
        even, odd = pair[:, :, :, 0].reshape(m, rows, half), pair[:, :, :, 1].reshape(m, rows, half)
        return jnp.concatenate([jnp.where(first, even, odd), jnp.where(first, odd, even)], axis=-1)

    def kernel(core_ref, src, out):
        for core in range(2):

            @pl.when(core_ref[0] == core)
            def _():
                for i in range(count):
                    for r in range(2):
                        apart = pl.ds(r * half + i * block, block)
                        mixed = pl.ds((2 * i + (core ^ r)) * block, block)
                        if back:
                            out[:, mixed] = src[:, apart]
                        else:
                            out[:, apart] = src[:, mixed]

    step = 128
    total = m * rows
    out = pl.pallas_call(
        kernel,
        out_shape=jax.ShapeDtypeStruct((total, width), a.dtype),
        grid_spec=pltpu.PrefetchScalarGridSpec(
            num_scalar_prefetch=1,
            grid=(total // step,),
            in_specs=[pl.BlockSpec((step, width), lambda i, core: (i, 0))],
            out_specs=pl.BlockSpec((step, width), lambda i, core: (i, 0)),
        ),
        cost_estimate=pl.CostEstimate(
            flops=0, bytes_accessed=2 * total * width * a.dtype.itemsize, transcendentals=0
        ),
    )(c.reshape(1).astype(jnp.int32), a.reshape(total, width))
    return out.reshape(a.shape)


def reduce_z(grad, z, y):
    bit = 1
    for _ in far_bits():
        n, _, block, cols = grad.shape
        pairs = grad.reshape(n // 2, 2, 2, block, cols)
        here = (z // bit) % 2
        got = swap_z(pick(pairs, 1, 1 - here).astype(BF), bit)
        grad = pick(pairs, 1, here) + got.astype(F32)
        bit *= 2
    mine = pick(grad[0], 0, y)
    return mine, swap_y(pick(grad[0], 0, 1 - y).astype(BF)).astype(F32)


def join(parts, y):
    mine, got = parts
    first = y == 0
    return jnp.concatenate([jnp.where(first, mine, got), jnp.where(first, got, mine)], axis=1)


def rows_rows(left, right):
    return lax.dot_general(left, right, (((0,), (0,)), ((), ())), preferred_element_type=F32)


def cols_cols(left, right):
    return lax.dot_general(left, right, (((1,), (1,)), ((), ())), preferred_element_type=F32)


def rotate(v, cos, sin):
    half = v.shape[-1] // 2
    turned = jnp.concatenate([-v[..., half:], v[..., :half]], axis=-1)
    return v * cos + turned * sin


def rotate_back(v, cos, sin):
    half = v.shape[-1] // 2
    w = v * sin
    turned = jnp.concatenate([w[..., half:], -w[..., :half]], axis=-1)
    return v * cos + turned


def norm_back(d_normed, unit, gain, scale):
    d_unit = d_normed * gain
    return scale * (d_unit - unit * jnp.mean(d_unit * unit, axis=-1, keepdims=True))


def on_device(
    hidden_in,
    segment_ids,
    attn_gain,
    mlp_gain,
    w_query,
    key_weight,
    value_weight,
    w_out,
    w_gate,
    w_up,
    w_down,
    out_cotangent,
):
    z, y, c, x = (lax.axis_index(n) for n in ("z", "y", "c", "x"))
    nz = lax.axis_size("z")
    micro = hidden_in.shape[0]
    toks = hidden_in.shape[2]
    width = hidden_in.shape[3]
    block = w_query.shape[0]
    scale = HEAD_SIZE ** (-0.5)
    extra = 16

    def pack_attn(index):
        gains = jnp.stack([attn_gain, mlp_gain])
        body = jnp.concatenate(
            [
                column_part(w_query, index),
                column_part(key_weight, index),
                column_part(value_weight, index),
                column_part(w_out, index),
            ],
            axis=1,
        )
        gains = jnp.pad(gains, ((0, extra - 2), (0, body.shape[1] - block)))
        return jnp.concatenate([body, gains], axis=0)

    def pack_gu(index):
        return jnp.concatenate([column_part(w_gate, index), column_part(w_up, index)], axis=1)

    def pack_down(index):
        return column_part(w_down, index)

    q_cols = w_query.shape[1] // 2
    kv_cols = key_weight.shape[1] // 2
    qkv_cols = q_cols + 2 * kv_cols
    own_far = z_first(pack_attn(y))
    attn_theirs = swap_y(pack_attn(1 - y))
    other_ids = swap_y(segment_ids[:, 0])
    attn_theirs, other_ids, hid, *own_far = meet(attn_theirs, other_ids, hidden_in[:, 0], *own_far)
    peer_far = z_first(attn_theirs)
    hid = regroup(hid, block, c)
    hid_near = gather_near(hid)
    attn_own = z_rest(own_far)
    more = meet(*hid_near, *peer_far, pack_gu(y), pack_gu(1 - y))
    hid_near, peer_far, gu_mine, gu_give = more[:3], more[3:5], more[5], more[6]
    hid_diag = gather_diag(hid_near)
    attn_peer = z_rest(peer_far)
    gu_far = z_first(gu_mine)
    more = meet(out_cotangent[:, 0], pack_down(1 - y), gu_give, *hid_diag, *attn_own, *attn_peer, *gu_far)
    cot, down_give, gu_give, hid_diag = *more[:3], more[3:5]
    attn_own, attn_peer, gu_far = both(more[5:7])[:, 0], both(more[7:9])[:, 0], more[9:]
    attn_streams = (attn_own, swap_c(attn_own), attn_peer, swap_c(attn_peer))
    gu_theirs = swap_y(gu_give)
    hid_all = gather_join(hid_near, hid_diag)
    attn_w = assemble(attn_streams, z, y, extra, (qkv_cols,))
    qkv_w, out_w, gains = attn_w
    qkv_w, out_w = qkv_w.reshape(width, -1), out_w.reshape(width, -1)
    gains = gains[:, :, :, :2, :block].astype(F32)
    gain_a = gains[:, :, :, 0].reshape(width)
    gain_m = gains[:, :, :, 1].reshape(width)
    hid_all, gu_theirs, qkv_w, out_w, gain_a, gain_m = meet(hid_all, gu_theirs, qkv_w, out_w, gain_a, gain_m)
    gu_own = z_rest(gu_far)
    gu_far = z_first(gu_theirs)
    down_theirs = swap_y(down_give)
    cot = regroup(cot, block, c)
    cot_near = gather_near(cot)

    length = 2 * toks
    groups = micro * 2
    ids = jnp.stack([segment_ids[:, 0], other_ids], axis=1).reshape(groups, length)
    ids = jnp.where(x == 0, ids, jnp.roll(ids, toks, axis=1))
    pos = (jnp.arange(length, dtype=jnp.int32) + toks * x) % length
    same = ids[:, :, None] == ids[:, None, :]
    allowed = jnp.logical_and(same, (pos[None, :] <= pos[:, None])[None])
    places = jnp.sum(allowed.astype(F32), axis=2) - 1.0
    freq = jnp.arange(HEAD_SIZE // 2, dtype=F32)
    inverse = 10000.0 ** (-2.0 * freq / HEAD_SIZE)
    angles = places[:, :, None] * inverse
    cos = jnp.concatenate([jnp.cos(angles)] * 2, axis=-1)
    sin = jnp.concatenate([jnp.sin(angles)] * 2, axis=-1)

    rows = micro * 4 * toks
    heads = q_cols // HEAD_SIZE

    def attention(hid_all, gain_a, qkv_w, out_w, cos, sin, allowed):
        hid32 = hid_all.astype(F32).reshape(rows, width)
        scale_a = lax.rsqrt(jnp.mean(hid32 * hid32, axis=-1, keepdims=True) + EPS)
        normed_a = (hid32 * scale_a * gain_a).astype(BF)
        qkv = jnp.dot(normed_a, qkv_w, preferred_element_type=F32)
        q_lin = qkv[:, :q_cols].reshape(groups, length, heads, HEAD_SIZE)
        k_lin = qkv[:, q_cols : q_cols + kv_cols].reshape(groups, length, HEAD_SIZE)
        values = qkv[:, q_cols + kv_cols :].astype(BF).reshape(groups, length, HEAD_SIZE)
        queries = rotate(q_lin, cos[:, :, None], sin[:, :, None]).astype(BF)
        keys = rotate(k_lin, cos, sin).astype(BF)
        scores = jnp.einsum("gqhd,gsd->ghqs", queries, keys, preferred_element_type=F32) * scale
        scores = jnp.where(allowed[:, None], scores, -1e30)
        top = jnp.max(scores, axis=-1, keepdims=True)
        expo = jnp.exp(scores - top)
        probs = expo / jnp.sum(expo, axis=-1, keepdims=True)
        attended = jnp.einsum("ghqs,gsd->gqhd", probs.astype(BF), values, preferred_element_type=F32)
        attended = attended.reshape(rows, q_cols).astype(BF)
        attn_part = cols_cols(attended, out_w).astype(BF).reshape(micro, 4 * toks, width)
        return scale_a, normed_a, queries, keys, values, probs, attended, attn_part

    scale_a, normed_a, queries, keys, values, probs, attended, attn_part = single(
        attention, hid_all, gain_a, qkv_w, out_w, cos, sin, allowed
    )
    more = meet(attn_part, down_theirs, pack_down(y), *cot_near, *gu_own, *gu_far)
    attn_part, down_theirs, down_mine, cot_near = *more[:3], more[3:6]
    gu_own, gu_far = more[6:8], more[8:]
    attn_far = scatter_far(attn_part)
    gu_peer = z_rest(gu_far)
    down_far = z_first(down_mine, down_theirs)
    attn_near = scatter_near(*scatter_prep(attn_part, attn_far))
    more = meet(*attn_near, *gu_peer, *down_far, *gu_own, *cot_near)
    attn_near, gu_peer, down_far, gu_own = more[:2], both(more[2:4])[:, 0], more[4:6], both(more[6:8])[:, 0]
    cot_near = more[8:]
    mid = hid.astype(F32) + scatter_sum(attn_part, attn_near)

    scale_m = lax.rsqrt(jnp.mean(mid * mid, axis=-1, keepdims=True) + EPS)
    unit_m = mid * scale_m
    normed_near = gather_near((unit_m * gain_m).astype(BF))
    down = z_rest(down_far)
    gu_streams = (gu_own, swap_c(gu_own), gu_peer, swap_c(gu_peer))
    more = meet(*gu_streams, *down, *normed_near, *cot_near)
    gu_streams, down, normed_near, cot_near = more[:4], both(more[4:6]), more[6:9], more[9:]
    normed_m = gather_far(normed_near).reshape(rows, width)
    cot_diag = gather_diag(cot_near)
    gu_w = assemble(gu_streams, z, y)[0].reshape(width, -1)
    down_c = swap_c(down)
    normed_m, gu_w, *cot_diag = meet(normed_m, gu_w, *cot_diag)
    cot_rows = gather_join(cot_near, cot_diag).reshape(rows, width)

    def feed(normed_m, gu_w, cot_rows):
        gu = jnp.dot(normed_m, gu_w, preferred_element_type=F32)
        ff = gu.shape[1] // 2
        inner = (jax.nn.silu(gu[:, :ff]) * gu[:, ff:]).astype(BF)
        return gu, inner, grad_half(1, cot_rows, inner)

    gu, inner, down_send = single(feed, normed_m, gu_w, cot_rows)
    down_send, down_c = meet(down_send, down_c)
    down_got = swap_c(down_send)
    down_w = assemble((down[:, 0], down_c[:, 0], down[:, 1], down_c[:, 1]), z, y)[0].reshape(width, -1)

    def feed_back(gu, inner, cot_rows, down_w, gu_w):
        d_inner = jnp.dot(cot_rows, down_w, preferred_element_type=F32)
        ff = gu.shape[1] // 2
        gate, up = gu[:, :ff], gu[:, ff:]
        sig = jax.nn.sigmoid(gate)
        d_gate = (d_inner * up * sig * (1.0 + gate * (1.0 - sig))).astype(BF)
        d_up = (d_inner * gate * sig).astype(BF)
        d_gu = jnp.concatenate([d_gate, d_up], axis=1)
        back = cols_cols(d_gu, gu_w).astype(BF)
        return d_gate, d_up, back.reshape(micro, 4 * toks, width), grad_half(0, cot_rows, inner)

    d_gate, d_up, back_mlp, down_keep = single(feed_back, gu, inner, cot_rows, down_w, gu_w)
    back_mlp, down_keep, down_got = meet(back_mlp, down_keep, down_got)
    back_far = scatter_far(back_mlp)

    def gate_grads(normed_m, d_gate):
        return grad_half(1, normed_m, d_gate), grad_half(0, normed_m, d_gate)

    gate_send, gate_keep = single(gate_grads, normed_m, d_gate)
    gate_send, gate_keep, *back_far = meet(gate_send, gate_keep, *back_far)
    gate_got = swap_c(gate_send)
    *ready, d_up, gate_keep, gate_got = meet(*scatter_prep(back_mlp, back_far), d_up, gate_keep, gate_got)
    back_near = scatter_near(*ready)
    down_sum = reduce_near((down_keep, down_got), z)
    gate_sum = reduce_near((gate_keep, gate_got), z)

    def up_grads(normed_m, d_up, inner, down_w):
        part = cols_cols(inner, down_w).astype(BF).reshape(micro, 4 * toks, width)
        return grad_half(1, normed_m, d_up), grad_half(0, normed_m, d_up), part

    up_send, up_keep, mlp_part = single(up_grads, normed_m, d_up, inner, down_w)
    up_send, up_keep, mlp_part, *back_near = meet(up_send, up_keep, mlp_part, *back_near)
    up_got = swap_c(up_send)
    d_normed_m = scatter_sum(back_mlp, back_near)
    gain_m_part = jnp.sum(d_normed_m * unit_m, axis=(0, 1))
    d_mid = cot.astype(F32) + norm_back(d_normed_m, unit_m, gain_m, scale_m)

    d_mid_near = gather_near(d_mid.astype(BF))
    more = meet(up_keep, up_got, *d_mid_near, *down_sum, *gate_sum)
    up_keep, up_got, d_mid_near, down_sum, gate_sum = *more[:2], more[2:5], more[5:7], more[7:]
    d_mid_diag = gather_diag(d_mid_near)
    up_sum = reduce_near((up_keep, up_got), z)
    down_sum = reduce_far(down_sum, z)
    more = meet(mlp_part, *d_mid_diag, *d_mid_near)
    mlp_part, d_mid_diag, d_mid_near = more[0], more[1:3], more[3:]
    gate_sum = reduce_far(gate_sum, z)
    mlp_far = scatter_far(mlp_part)
    d_mid_all = gather_join(d_mid_near, d_mid_diag).reshape(rows, width)

    def attention_back(d_mid_all, out_w, values, probs, attended):
        d_att = jnp.dot(d_mid_all, out_w, preferred_element_type=F32).astype(BF)
        d_att = d_att.reshape(groups, length, heads, HEAD_SIZE)
        d_probs = jnp.einsum("gqhd,gsd->ghqs", d_att, values, preferred_element_type=F32)
        inner_sum = jnp.sum(probs * d_probs, axis=-1, keepdims=True)
        d_scores = (probs * (d_probs - inner_sum)).astype(BF)
        return d_att, d_scores, grad_half(1, d_mid_all, attended), grad_half(0, d_mid_all, attended)

    d_att, d_scores, out_send, out_keep = single(attention_back, d_mid_all, out_w, values, probs, attended)
    d_scores, out_send, out_keep, *more = meet(d_scores, out_send, out_keep, *mlp_far, *up_sum, *down_sum)
    mlp_far, up_sum, down_sum = more[:2], more[2:4], more[4:]
    out_got = swap_c(out_send)
    down_parts = reduce_y(down_sum, y)
    up_sum = reduce_far(up_sum, z)
    mlp_near = scatter_near(*scatter_prep(mlp_part, mlp_far))
    out_sum = reduce_near((out_keep, out_got), z)

    def qkv_back(d_scores, d_att, probs, queries, keys, cos, sin, qkv_w, hid_all, scale_a):
        d_queries = jnp.einsum("ghqs,gsd->gqhd", d_scores, keys, preferred_element_type=F32) * scale
        d_keys = jnp.einsum("ghqs,gqhd->gsd", d_scores, queries, preferred_element_type=F32) * scale
        d_values = jnp.einsum("ghqs,gqhd->gsd", probs.astype(BF), d_att, preferred_element_type=F32)
        d_q = rotate_back(d_queries, cos[:, :, None], sin[:, :, None]).reshape(rows, q_cols)
        d_k = rotate_back(d_keys, cos, sin).reshape(rows, kv_cols)
        d_v = d_values.reshape(rows, kv_cols)
        d_qkv = jnp.concatenate([d_q, d_k, d_v], axis=1).astype(BF)
        back = cols_cols(d_qkv, qkv_w)
        unit_a = hid_all.astype(F32).reshape(rows, width) * scale_a
        return d_qkv, back.astype(BF).reshape(micro, 4 * toks, width), jnp.sum(back * unit_a, axis=0)

    d_qkv, back_attn, gain_a_part = single(
        qkv_back, d_scores, d_att, probs, queries, keys, cos, sin, qkv_w, hid_all, scale_a
    )
    gain_rows = jnp.stack([gain_a_part, gain_m_part]).reshape(2, 2, nz, 2, block)
    gain_rows = gain_rows.transpose(1, 2, 3, 0, 4)
    gain_rows = jnp.pad(gain_rows, ((0, 0),) * 3 + ((0, extra - 2), (0, qkv_cols - block))).astype(BF)
    qkv_send = jnp.concatenate([grad_half(1, normed_a, d_qkv), gain_rows[1]], axis=2)
    back_attn, qkv_send, d_qkv, *more = meet(
        back_attn, qkv_send, d_qkv, *mlp_near, *gate_sum, *up_sum, *out_sum
    )
    mlp_near, gate_sum, up_sum, out_sum = more[:2], more[2:4], more[4:6], more[6:]
    qkv_got = swap_c(qkv_send)
    attn_far = scatter_far(back_attn)
    qkv_keep = jnp.concatenate([grad_half(0, normed_a, d_qkv), gain_rows[0]], axis=2)
    qkv_keep, qkv_got = meet(qkv_keep, qkv_got)
    qkv_sum = reduce_near((qkv_keep, qkv_got), z)
    more = meet(*attn_far, *qkv_sum)
    attn_far, qkv_sum = more[:2], more[2:]
    attn_near = scatter_near(*scatter_prep(back_attn, attn_far))
    qkv_sum = reduce_far(qkv_sum, z)
    out_sum = reduce_far(out_sum, z)
    attn_near0, attn_near1, *more = meet(*attn_near, *qkv_sum, *out_sum, *mlp_near, *gate_sum, *up_sum)
    attn_near, qkv_sum, out_sum = (attn_near0, attn_near1), more[:2], more[2:4]
    mlp_near, gate_sum, up_sum = more[4:6], more[6:8], more[8:]
    qkv_parts = reduce_y(qkv_sum, y)
    gate_parts = reduce_y(gate_sum, y)
    up_parts = reduce_y(up_sum, y)
    out_parts = reduce_y(out_sum, y)
    block_out = (mid + scatter_sum(mlp_part, mlp_near)).astype(BF)
    d_normed_a = scatter_sum(back_attn, attn_near)
    sc_a = scale_a.reshape(micro, 4 * toks, 1)[:, :toks]
    unit_a = hid.astype(F32) * sc_a
    input_grad = d_mid + norm_back(d_normed_a, unit_a, gain_a, sc_a)

    keep = (qkv_parts[0] + qkv_parts[1])[block : block + 2, :block]
    keep = keep + swap_x(keep)
    qkv_parts = tuple(p[:block] for p in qkv_parts)

    def cut(parts, lo, hi):
        return join((parts[0][:, lo:hi], parts[1][:, lo:hi]), y)

    return (
        regroup(block_out, block, c, True)[:, None],
        regroup(input_grad, block, c, True)[:, None],
        keep[0],
        keep[1],
        cut(qkv_parts, 0, q_cols),
        cut(qkv_parts, q_cols, q_cols + kv_cols),
        cut(qkv_parts, q_cols + kv_cols, qkv_cols),
        join(out_parts, y),
        join(gate_parts, y),
        join(up_parts, y),
        join(down_parts, y),
    )


def solution(mesh):
    n_dp, n_tensor = mesh.shape["dp"], mesh.shape["tensor"]
    grid = Mesh(mesh.devices.reshape(n_dp // 4, 2, 2, n_tensor), ("z", "y", "c", "x"))
    dp = ("z", "y", "c")
    token = P(None, dp, "x", None)
    weight = P(dp, "x")
    gain = P(dp)
    in_specs = (token, P(None, dp, None), gain, gain) + (weight,) * 7 + (token,)
    out_specs = (token, token, gain, gain) + (weight,) * 7
    return jax.shard_map(
        on_device, mesh=grid, in_specs=in_specs, out_specs=out_specs, check_vma=False
    )
```

```python
import jax
import jax.numpy as jnp
import numpy as np
from jax import lax
from jax.experimental import pallas as pl
from jax.experimental.pallas import tpu as pltpu
from jax.sharding import Mesh
from jax.sharding import PartitionSpec as P

HEAD_SIZE = 64
EPS = 1e-05
BF = jnp.bfloat16
F32 = jnp.float32


def swap_x(a):
    return lax.ppermute(a, "x", [(0, 1), (1, 0)])


def swap_y(a):
    return lax.ppermute(a, "y", [(0, 1), (1, 0)])


def swap_c(a):
    return lax.ppermute(a, "c", [(0, 1), (1, 0)])


def swap_z(a, bit):
    n = lax.axis_size("z")
    return lax.ppermute(a, "z", [(i, i ^ bit) for i in range(n)])


def far_bits():
    n = lax.axis_size("z")
    bits = []
    bit = n // 2
    while bit:
        bits.append(bit)
        bit //= 2
    return bits


def z_order():
    order = [0]
    for bit in far_bits():
        order = order + [r ^ bit for r in order]
    return order


def meet(*values):
    return lax.optimization_barrier(values)


def single(work, *args):
    shapes = jax.eval_shape(work, *args)
    return lax.cond(
        lax.axis_index("z") >= 0,
        work,
        lambda *_: jax.tree.map(lambda s: jnp.zeros(s.shape, s.dtype), shapes),
        *args,
    )


def gather_near(own):
    return own, swap_x(own), swap_y(own)


def diag_parts(near):
    half = near[1].shape[-1] // 2
    return near[1][..., :half], near[2][..., half:]


def gather_diag(parts):
    return swap_y(parts[0]), swap_x(parts[1])


def gather_join(near, diag):
    return jnp.concatenate(tuple(near) + (jnp.concatenate(diag, axis=-1),), axis=1)


def far_parts(part):
    m, rows, f = part.shape
    diag = part[:, 3 * rows // 4 :]
    return diag[..., : f // 2], diag[..., f // 2 :]


def scatter_far(parts):
    return swap_y(parts[0]), swap_x(parts[1])


def scatter_prep(part, far):
    m, rows, f = part.shape
    half = f // 2
    low, high = far
    part = part.reshape(m, 4, rows // 4, f)
    to_x = part[:, 1]
    to_y = part[:, 2]
    to_x = jnp.concatenate(
        [(to_x[..., :half].astype(F32) + low.astype(F32)).astype(BF), to_x[..., half:]], axis=-1
    )
    to_y = jnp.concatenate(
        [to_y[..., :half], (to_y[..., half:].astype(F32) + high.astype(F32)).astype(BF)], axis=-1
    )
    return to_x, to_y


def scatter_near(to_x, to_y):
    return swap_x(to_x), swap_y(to_y)


def scatter_sum(part, near):
    rows = part.shape[1] // 4
    return part[:, :rows].astype(F32) + near[0].astype(F32) + near[1].astype(F32)


def column_part(a, index):
    width = a.shape[1] // 2
    return lax.dynamic_slice_in_dim(a, index * width, width, axis=1)


def pick(a, axis, index):
    return lax.dynamic_index_in_dim(a, index, axis, keepdims=False)


def z_first(*shards):
    held = jnp.stack(shards)[None]
    return held, swap_z(held, far_bits()[0])


def z_lead(pair):
    bits = far_bits()[1:-1]
    if not bits:
        return pair
    held = jnp.concatenate(pair, axis=0)
    for bit in bits:
        held = jnp.concatenate([held, swap_z(held, bit)], axis=0)
    half = held.shape[0] // 2
    return held[:half], held[half:]


def z_rest(pair):
    held = jnp.concatenate(z_lead(pair), axis=0)
    return held, swap_z(held, 1)


def both(pair):
    return jnp.concatenate(pair, axis=0)


def assemble(streams, z, y, extra=0, split=()):
    order = np.array(z_order() + [0], np.int32)
    n, _, rows, cols = streams[0][0].shape
    block = rows - extra
    last = np.arange(n + 1) == n
    where = jnp.where(jnp.asarray(last), y, jnp.asarray(order) ^ z)

    edges = (0,) + tuple(split) + (cols,)
    spans = list(zip(edges[:-1], edges[1:]))

    def kernel(where_ref, own, own_c, peer, peer_c, *more):
        yy = where_ref[n]
        for ref, at_c, at_y in ((own, 0, yy), (own_c, 1, yy), (peer, 0, 1 - yy), (peer_c, 1, 1 - yy)):
            if not extra:
                more[0][at_c, 0, at_y] = ref[0, 0]
                continue
            for out, (lo, hi) in zip(more, spans):
                out[at_c, 0, at_y] = ref[0, 0, :block, lo:hi]
            more[-1][at_c, 0, at_y] = ref[0, 0, block:, :128]

    out_shape = [jax.ShapeDtypeStruct((2, n, 2, block, hi - lo), BF) for lo, hi in spans]
    out_specs = [
        pl.BlockSpec((2, 1, 2, block, hi - lo), lambda i, at: (0, at[i], 0, 0, 0)) for lo, hi in spans
    ]
    if extra:
        out_shape.append(jax.ShapeDtypeStruct((2, n, 2, extra, 128), BF))
        out_specs.append(pl.BlockSpec((2, 1, 2, extra, 128), lambda i, at: (0, at[i], 0, 0, 0)))
    moved = 4 * n * rows * cols * 4
    return pl.pallas_call(
        kernel,
        out_shape=out_shape,
        grid_spec=pltpu.PrefetchScalarGridSpec(
            num_scalar_prefetch=1,
            grid=(n,),
            in_specs=[
                pl.BlockSpec((1, 1, rows, cols), lambda i, at, k=k: (i, k, 0, 0)) for _, k in streams
            ],
            out_specs=out_specs,
        ),
        cost_estimate=pl.CostEstimate(flops=0, bytes_accessed=moved, transcendentals=0),
    )(where, *(s for s, _ in streams))


def grad_half(index, left, right):
    nz = lax.axis_size("z")
    half = left.shape[1] // 2
    part = rows_rows(left[:, index * half : (index + 1) * half], right).astype(BF)
    return part.reshape(nz, 2, half // (2 * nz), right.shape[1])


def add(a, b):
    return a.astype(F32) + b.astype(F32)


def halve(pair, z, bit):
    n, _, block, cols = pair[0].shape
    pairs = [p.reshape(n // 2, 2, 2, block, cols) for p in pair]
    here = (z // bit) % 2
    keep = add(*(pick(p, 1, here) for p in pairs))
    send = add(*(pick(p, 1, 1 - here) for p in pairs))
    return keep, send.astype(pair[1].dtype)


def halve_near(pair, z):
    return halve(pair, z, 1)


def far_last():
    return far_bits()[0]


def far_steps(pair, z):
    for bit in far_bits()[1:-1][::-1]:
        pair = swapped(halve(pair, z, bit), bit)
    return pair


def halve_far(pair, z):
    return halve(far_steps(pair, z), z, far_last())


def swapped(halves, bit):
    return halves[0], swap_z(halves[1], bit)


def reduce_y(pair, y):
    keep, send = (add(*(pick(p[0], 0, at) for p in pair)) for at in (y, 1 - y))
    return keep, swap_y(send.astype(pair[1].dtype))


def side_by_side(low, high):
    return tuple(jnp.concatenate(p, axis=-1) for p in zip(low, high))


def columns(halves, lo, hi):
    return tuple(h[..., lo:hi] for h in halves)


def join(parts, y):
    mine, got = parts[0], parts[1].astype(F32)
    first = y == 0
    return jnp.concatenate([jnp.where(first, mine, got), jnp.where(first, got, mine)], axis=1)


def regroup(a, block, c, back=False):
    m, rows, width = a.shape
    half = width // 2
    count = half // block
    if block % 128:
        first = c == 0
        if back:
            own, other = (p.reshape(m, rows, count, block) for p in (a[..., :half], a[..., half:]))
            pair = jnp.stack([jnp.where(first, own, other), jnp.where(first, other, own)], axis=3)
            return pair.reshape(m, rows, width)
        pair = a.reshape(m, rows, count, 2, block)
        even, odd = pair[:, :, :, 0].reshape(m, rows, half), pair[:, :, :, 1].reshape(m, rows, half)
        return jnp.concatenate([jnp.where(first, even, odd), jnp.where(first, odd, even)], axis=-1)

    def kernel(core_ref, src, out):
        for core in range(2):

            @pl.when(core_ref[0] == core)
            def _():
                for i in range(count):
                    for r in range(2):
                        apart = pl.ds(r * half + i * block, block)
                        mixed = pl.ds((2 * i + (core ^ r)) * block, block)
                        if back:
                            out[:, mixed] = src[:, apart]
                        else:
                            out[:, apart] = src[:, mixed]

    step = 128
    total = m * rows
    out = pl.pallas_call(
        kernel,
        out_shape=jax.ShapeDtypeStruct((total, width), a.dtype),
        grid_spec=pltpu.PrefetchScalarGridSpec(
            num_scalar_prefetch=1,
            grid=(total // step,),
            in_specs=[pl.BlockSpec((step, width), lambda i, core: (i, 0))],
            out_specs=pl.BlockSpec((step, width), lambda i, core: (i, 0)),
        ),
        cost_estimate=pl.CostEstimate(
            flops=0, bytes_accessed=2 * total * width * a.dtype.itemsize, transcendentals=0
        ),
    )(c.reshape(1).astype(jnp.int32), a.reshape(total, width))
    return out.reshape(a.shape)


def reduce_z(grad, z, y):
    bit = 1
    for _ in far_bits():
        n, _, block, cols = grad.shape
        pairs = grad.reshape(n // 2, 2, 2, block, cols)
        here = (z // bit) % 2
        got = swap_z(pick(pairs, 1, 1 - here).astype(BF), bit)
        grad = pick(pairs, 1, here) + got.astype(F32)
        bit *= 2
    mine = pick(grad[0], 0, y)
    return mine, swap_y(pick(grad[0], 0, 1 - y).astype(BF)).astype(F32)


def rows_rows(left, right):
    return lax.dot_general(left, right, (((0,), (0,)), ((), ())), preferred_element_type=F32)


def cols_cols(left, right):
    return lax.dot_general(left, right, (((1,), (1,)), ((), ())), preferred_element_type=F32)


def rotate(v, cos, sin):
    half = v.shape[-1] // 2
    turned = jnp.concatenate([-v[..., half:], v[..., :half]], axis=-1)
    return v * cos + turned * sin


def rotate_back(v, cos, sin):
    half = v.shape[-1] // 2
    w = v * sin
    turned = jnp.concatenate([w[..., half:], -w[..., :half]], axis=-1)
    return v * cos + turned


def norm_back(d_normed, unit, gain, scale):
    d_unit = d_normed * gain
    return scale * (d_unit - unit * jnp.mean(d_unit * unit, axis=-1, keepdims=True))


def on_device(
    hidden_in,
    segment_ids,
    attn_gain,
    mlp_gain,
    w_query,
    key_weight,
    value_weight,
    w_out,
    w_gate,
    w_up,
    w_down,
    out_cotangent,
):
    z, y, c, x = (lax.axis_index(n) for n in ("z", "y", "c", "x"))
    nz = lax.axis_size("z")
    micro = hidden_in.shape[0]
    toks = hidden_in.shape[2]
    width = hidden_in.shape[3]
    block = w_query.shape[0]
    scale = HEAD_SIZE ** (-0.5)
    extra = 16

    def pack_attn(index):
        gains = jnp.stack([attn_gain, mlp_gain])
        body = jnp.concatenate(
            [
                column_part(w_query, index),
                column_part(key_weight, index),
                column_part(value_weight, index),
                column_part(w_out, index),
            ],
            axis=1,
        )
        gains = jnp.pad(gains, ((0, extra - 2), (0, body.shape[1] - block)))
        return jnp.concatenate([body, gains], axis=0)

    def pack_gu(index):
        return jnp.concatenate([column_part(w_gate, index), column_part(w_up, index)], axis=1)

    def pack_down(index):
        return column_part(w_down, index)

    q_cols = w_query.shape[1] // 2
    kv_cols = key_weight.shape[1] // 2
    qkv_cols = q_cols + 2 * kv_cols
    own_far = z_first(pack_attn(y))
    attn_theirs = swap_y(pack_attn(1 - y))
    other_ids = swap_y(segment_ids[:, 0])
    own_far, attn_theirs, other_ids, hid = meet(own_far, attn_theirs, other_ids, hidden_in[:, 0])
    peer_far = z_first(attn_theirs)
    attn_own = z_rest(own_far)
    hid = regroup(hid, block, c)
    hid_near = gather_near(hid)
    peer_far, attn_own, hid_near, hid_parts, gu_mine, gu_give = meet(
        peer_far, attn_own, hid_near, diag_parts(hid_near), pack_gu(y), pack_gu(1 - y)
    )
    attn_peer = z_rest(peer_far)
    gu_far = z_first(gu_mine)
    hid_diag = gather_diag(hid_parts)
    gu_theirs = swap_y(gu_give)
    attn_own = both(attn_own)
    cot = regroup(out_cotangent[:, 0], block, c)
    attn_peer, gu_far, hid_diag, gu_theirs, attn_own, cot, down_give = meet(
        attn_peer, gu_far, hid_diag, gu_theirs, attn_own, cot, pack_down(1 - y)
    )
    attn_own_c = swap_c(attn_own)
    attn_peer = both(attn_peer)
    attn_peer_c = swap_c(attn_peer)
    hid_all = gather_join(hid_near, hid_diag)
    gu_own = z_rest(gu_far)
    gu_peer = z_first(gu_theirs)
    cot_near = gather_near(cot)
    down_theirs = swap_y(down_give)
    attn_streams = ((attn_own, 0), (attn_own_c, 0), (attn_peer, 0), (attn_peer_c, 0))
    qkv_w, out_w, gains = assemble(attn_streams, z, y, extra, (qkv_cols,))
    qkv_w, out_w = qkv_w.reshape(width, -1), out_w.reshape(width, -1)
    gains = gains[:, :, :, :2, :block].astype(F32)
    gain_a = gains[:, :, :, 0].reshape(width)
    gain_m = gains[:, :, :, 1].reshape(width)

    length = 2 * toks
    groups = micro * 2
    ids = jnp.stack([segment_ids[:, 0], other_ids], axis=1).reshape(groups, length)
    ids = jnp.where(x == 0, ids, jnp.roll(ids, toks, axis=1))
    pos = (jnp.arange(length, dtype=jnp.int32) + toks * x) % length
    same = ids[:, :, None] == ids[:, None, :]
    allowed = jnp.logical_and(same, (pos[None, :] <= pos[:, None])[None])
    places = jnp.sum(allowed.astype(F32), axis=2) - 1.0
    freq = jnp.arange(HEAD_SIZE // 2, dtype=F32)
    inverse = 10000.0 ** (-2.0 * freq / HEAD_SIZE)
    angles = places[:, :, None] * inverse
    cos = jnp.concatenate([jnp.cos(angles)] * 2, axis=-1)
    sin = jnp.concatenate([jnp.sin(angles)] * 2, axis=-1)

    rows = micro * 4 * toks
    heads = q_cols // HEAD_SIZE

    def attention(hid_all, gain_a, qkv_w, out_w, cos, sin, allowed):
        hid32 = hid_all.astype(F32).reshape(rows, width)
        scale_a = lax.rsqrt(jnp.mean(hid32 * hid32, axis=-1, keepdims=True) + EPS)
        normed_a = (hid32 * scale_a * gain_a).astype(BF)
        qkv = jnp.dot(normed_a, qkv_w, preferred_element_type=F32)
        q_lin = qkv[:, :q_cols].reshape(groups, length, heads, HEAD_SIZE)
        k_lin = qkv[:, q_cols : q_cols + kv_cols].reshape(groups, length, HEAD_SIZE)
        values = qkv[:, q_cols + kv_cols :].astype(BF).reshape(groups, length, HEAD_SIZE)
        queries = rotate(q_lin, cos[:, :, None], sin[:, :, None]).astype(BF)
        keys = rotate(k_lin, cos, sin).astype(BF)
        scores = jnp.einsum("gqhd,gsd->ghqs", queries, keys, preferred_element_type=F32) * scale
        scores = jnp.where(allowed[:, None], scores, -1e30)
        top = jnp.max(scores, axis=-1, keepdims=True)
        expo = jnp.exp(scores - top)
        probs = expo / jnp.sum(expo, axis=-1, keepdims=True)
        attended = jnp.einsum("ghqs,gsd->gqhd", probs.astype(BF), values, preferred_element_type=F32)
        attended = attended.reshape(rows, q_cols).astype(BF)
        attn_part = cols_cols(attended, out_w).astype(BF).reshape(micro, 4 * toks, width)
        return scale_a, normed_a, queries, keys, values, probs, attended, attn_part, far_parts(attn_part)

    scale_a, normed_a, queries, keys, values, probs, attended, attn_part, attn_far = single(
        attention, hid_all, gain_a, qkv_w, out_w, cos, sin, allowed
    )
    attn_part, attn_far, gu_own, gu_peer, cot_near, down_theirs, down_mine = meet(
        attn_part, attn_far, gu_own, gu_peer, cot_near, down_theirs, pack_down(y)
    )
    attn_far = scatter_far(attn_far)
    gu_lead = z_lead(gu_peer)
    gu_low = swap_z(gu_lead[0], 1)
    ready, gu_low, gu_own = meet(scatter_prep(attn_part, attn_far), gu_low, gu_own)
    attn_near = scatter_near(*ready)
    gu_high = swap_z(gu_lead[1], 1)
    down_own = z_first(down_mine)
    gu_own = both(gu_own)
    gu_own_c = swap_c(gu_own)
    attn_near, gu_high, down_own, gu_own_c = meet(attn_near, gu_high, down_own, gu_own_c)
    gu_peer = jnp.concatenate([*gu_lead, gu_low, gu_high], axis=0)
    mid = hid.astype(F32) + scatter_sum(attn_part, attn_near)

    scale_m = lax.rsqrt(jnp.mean(mid * mid, axis=-1, keepdims=True) + EPS)
    unit_m = mid * scale_m
    normed_near = gather_near((unit_m * gain_m).astype(BF))
    gu_peer_c = swap_c(gu_peer)
    down_peer = z_first(down_theirs)
    down_own = z_rest(down_own)
    normed_near, normed_parts, gu_peer_c, down_peer, down_own = meet(
        normed_near, diag_parts(normed_near), gu_peer_c, down_peer, down_own
    )
    normed_diag = gather_diag(normed_parts)
    down_peer = z_rest(down_peer)
    gu_streams = ((gu_own, 0), (gu_own_c, 0), (gu_peer, 0), (gu_peer_c, 0))
    gu_w = assemble(gu_streams, z, y)[0].reshape(width, -1)
    down_own = both(down_own)
    down_own_c = swap_c(down_own)
    normed_diag, down_peer, gu_w, down_own_c, cot_parts = meet(
        normed_diag, down_peer, gu_w, down_own_c, diag_parts(cot_near)
    )
    normed_m, cot_parts = meet(gather_join(normed_near, normed_diag).reshape(rows, width), cot_parts)
    cot_diag = gather_diag(cot_parts)

    def feed(normed_m, gu_w):
        gu = jnp.dot(normed_m, gu_w, preferred_element_type=F32)
        ff = gu.shape[1] // 2
        return gu, (jax.nn.silu(gu[:, :ff]) * gu[:, ff:]).astype(BF)

    gu, inner = single(feed, normed_m, gu_w)
    inner, cot_diag, down_peer = meet(inner, cot_diag, down_peer)
    down_peer = both(down_peer)
    down_peer_c = swap_c(down_peer)
    cot_rows = gather_join(cot_near, cot_diag).reshape(rows, width)
    down_got = swap_c(grad_half(1, cot_rows, inner))
    down_streams = ((down_own, 0), (down_own_c, 0), (down_peer, 0), (down_peer_c, 0))
    down_w = assemble(down_streams, z, y)[0].reshape(width, -1)
    down_keep = single(lambda a, b: grad_half(0, a, b), cot_rows, inner)
    gu, down_w, down_halves = meet(gu, down_w, halve_near((down_keep, down_got), z))
    down_sum = swapped(down_halves, 1)

    def feed_back(gu, cot_rows, down_w, gu_w):
        d_inner = jnp.dot(cot_rows, down_w, preferred_element_type=F32)
        ff = gu.shape[1] // 2
        gate, up = gu[:, :ff], gu[:, ff:]
        sig = jax.nn.sigmoid(gate)
        d_gate = (d_inner * up * sig * (1.0 + gate * (1.0 - sig))).astype(BF)
        d_up = (d_inner * gate * sig).astype(BF)
        d_gu = jnp.concatenate([d_gate, d_up], axis=1)
        back = cols_cols(d_gu, gu_w).astype(BF)
        back = back.reshape(micro, 4 * toks, width)
        return d_gate, d_up, back, far_parts(back)

    ff = inner.shape[1]
    cols = (ff // 256 + 1) * 128 if ff % 256 else ff // 2
    far = far_bits()[0]
    d_gate, d_up, back_mlp, back_far = single(feed_back, gu, cot_rows, down_w, gu_w)
    ff = d_gate.shape[1]
    cols = (ff // 256 + 1) * 128 if ff % 256 else ff // 2
    far = far_bits()[0]
    back_mlp, back_far, d_gate, down_sum = meet(back_mlp, back_far, d_gate, down_sum)
    back_far = scatter_far(back_far)

    def gate_grads(normed_m, d_gate):
        return grad_half(1, normed_m, d_gate), grad_half(0, normed_m, d_gate)

    gate_send, gate_keep = single(gate_grads, normed_m, d_gate)
    down_low = halve_far(columns(down_sum, 0, cols), z)
    down_high = halve_far(columns(down_sum, cols, ff), z)
    back_far, gate_send, gate_keep, down_low, down_high = meet(
        back_far, gate_send, gate_keep, down_low, down_high
    )
    gate_got = swap_c(gate_send)
    ready, gate_got = meet(scatter_prep(back_mlp, back_far), gate_got)
    back_near = scatter_near(*ready)
    down_low = swapped(down_low, far)
    gate_pair = gate_keep, gate_got
    d_up, gate_low, gate_high = meet(
        d_up, halve_near(columns(gate_pair, 0, cols), z), halve_near(columns(gate_pair, cols, ff), z)
    )
    gate_low = swapped(gate_low, 1)

    def up_grads(normed_m, d_up):
        return grad_half(1, normed_m, d_up), grad_half(0, normed_m, d_up)

    up_send, up_keep = single(up_grads, normed_m, d_up)
    back_near, down_low, gate_low, gate_high, down_high, up_send, up_keep = meet(
        back_near, down_low, gate_low, gate_high, down_high, up_send, up_keep
    )
    up_got = swap_c(up_send)

    def mid_back(back_mlp, from_x, from_y, unit_m, scale_m, gain_m, cot):
        d_normed_m = scatter_sum(back_mlp, (from_x, from_y))
        d_mid = cot.astype(F32) + norm_back(d_normed_m, unit_m, gain_m, scale_m)
        return d_mid, d_mid.astype(BF), jnp.sum(d_normed_m * unit_m, axis=(0, 1))

    d_mid, d_mid_low, gain_m_part = single(mid_back, back_mlp, *back_near, unit_m, scale_m, gain_m, cot)

    d_mid_low, up_got, inner = meet(d_mid_low, up_got, inner)
    d_mid_near = gather_near(d_mid_low)
    gate_high = swapped(gate_high, 1)
    down_high = swapped(down_high, far)

    def mlp_out(inner, down_w):
        part = cols_cols(inner, down_w).astype(BF).reshape(micro, 4 * toks, width)
        return part, far_parts(part)

    mlp_part, mlp_far = single(mlp_out, inner, down_w)
    up_pair = up_keep, up_got
    up_halves = halve_near(up_pair, z)
    gate_low = halve_far(gate_low, z)
    d_mid_near, d_mid_parts, gate_high, down_high, up_halves, gate_low, mlp_part = meet(
        d_mid_near, diag_parts(d_mid_near), gate_high, down_high, up_halves, gate_low, mlp_part
    )
    d_mid_diag = gather_diag(d_mid_parts)
    up_sum = swapped(up_halves, 1)
    gate_halves = side_by_side(gate_low, halve_far(gate_high, z))
    mlp_far, d_mid_diag, gate_halves, down_sum = meet(
        mlp_far, d_mid_diag, gate_halves, side_by_side(down_low, down_high)
    )
    d_mid_all = gather_join(d_mid_near, d_mid_diag).reshape(rows, width)
    mlp_far = scatter_far(mlp_far)
    gate_sum = swapped(gate_halves, far)
    down_parts = reduce_y(down_sum, y)

    def attention_back(d_mid_all, out_w, values, probs, attended):
        d_att = jnp.dot(d_mid_all, out_w, preferred_element_type=F32).astype(BF)
        d_att = d_att.reshape(groups, length, heads, HEAD_SIZE)
        d_probs = jnp.einsum("gqhd,gsd->ghqs", d_att, values, preferred_element_type=F32)
        inner_sum = jnp.sum(probs * d_probs, axis=-1, keepdims=True)
        d_scores = (probs * (d_probs - inner_sum)).astype(BF)
        return d_att, d_scores, grad_half(1, d_mid_all, attended), grad_half(0, d_mid_all, attended)

    d_att, d_scores, out_send, out_keep = single(attention_back, d_mid_all, out_w, values, probs, attended)
    d_scores, out_send, mlp_far, gate_sum, up_sum, down_parts = meet(
        d_scores, out_send, mlp_far, gate_sum, up_sum, down_parts
    )
    out_got = swap_c(out_send)
    d_scores, ready, up_halves, out_halves = meet(
        d_scores,
        scatter_prep(mlp_part, mlp_far),
        halve_far(up_sum, z),
        halve_near((out_keep, out_got), z),
    )
    mlp_near = scatter_near(*ready)
    up_sum = swapped(up_halves, far)
    out_sum = swapped(out_halves, 1)
    gate_parts = reduce_y(gate_sum, y)

    def qkv_back(d_scores, d_att, probs, queries, keys, cos, sin, qkv_w, hid_all, scale_a, gain_m_part):
        d_queries = jnp.einsum("ghqs,gsd->gqhd", d_scores, keys, preferred_element_type=F32) * scale
        d_keys = jnp.einsum("ghqs,gqhd->gsd", d_scores, queries, preferred_element_type=F32) * scale
        d_values = jnp.einsum("ghqs,gqhd->gsd", probs.astype(BF), d_att, preferred_element_type=F32)
        d_q = rotate_back(d_queries, cos[:, :, None], sin[:, :, None]).reshape(rows, q_cols)
        d_k = rotate_back(d_keys, cos, sin).reshape(rows, kv_cols)
        d_v = d_values.reshape(rows, kv_cols)
        d_qkv = jnp.concatenate([d_q, d_k, d_v], axis=1).astype(BF)
        back = cols_cols(d_qkv, qkv_w)
        unit_a = hid_all.astype(F32).reshape(rows, width) * scale_a
        gain_rows = jnp.stack([jnp.sum(back * unit_a, axis=0), gain_m_part]).reshape(2, 2, nz, 2, block)
        gain_rows = gain_rows.transpose(1, 2, 3, 0, 4)
        back = back.astype(BF).reshape(micro, 4 * toks, width)
        return d_qkv, back, far_parts(back), gain_rows[1], gain_rows[0]

    d_qkv, back_attn, attn_far, gain_send, gain_keep = single(
        qkv_back, d_scores, d_att, probs, queries, keys, cos, sin, qkv_w, hid_all, scale_a, gain_m_part
    )
    back_attn, attn_far, d_qkv, gain_send, mlp_near, out_sum, up_sum, gate_parts = meet(
        back_attn, attn_far, d_qkv, gain_send, mlp_near, out_sum, up_sum, gate_parts
    )
    attn_far = scatter_far(attn_far)
    gain_got = swap_c(gain_send)
    qkv_send = single(lambda a, b: grad_half(1, a, b), normed_a, d_qkv)
    d_qkv, qkv_send = meet(d_qkv, qkv_send)
    qkv_got = swap_c(qkv_send)

    def keep_halves(normed_a, d_qkv, out_sum):
        return grad_half(0, normed_a, d_qkv), halve(out_sum, z, far_last())

    qkv_keep, out_halves = single(keep_halves, normed_a, d_qkv, far_steps(out_sum, z))
    attn_far, qkv_got, gain_got, qkv_keep, out_halves = meet(attn_far, qkv_got, gain_got, qkv_keep, out_halves)

    def near_halves(back_attn, attn_far, qkv_pair, gain_pair):
        return scatter_prep(back_attn, attn_far), halve(qkv_pair, z, 1), halve(gain_pair, z, 1)

    ready, qkv_halves, gain_halves = single(
        near_halves, back_attn, attn_far, (qkv_keep, qkv_got), (gain_keep, gain_got)
    )
    mlp_near, ready, qkv_halves, gain_halves = meet(mlp_near, ready, qkv_halves, gain_halves)
    attn_near = scatter_near(*ready)
    qkv_sum, gain_sum = swapped(qkv_halves, 1), swapped(gain_halves, 1)
    out_sum = swapped(out_halves, far)

    def finish_out(mid, mlp_part, from_x, from_y):
        return (mid + scatter_sum(mlp_part, (from_x, from_y))).astype(BF)

    block_out = regroup(single(finish_out, mid, mlp_part, *mlp_near), block, c, True)
    qkv_sum, gain_sum, block_out = meet(qkv_sum, gain_sum, block_out)

    def far_halves(*pairs):
        return [halve(p, z, far_last()) for p in pairs]

    qkv_halves, gain_halves = single(far_halves, far_steps(qkv_sum, z), far_steps(gain_sum, z))
    attn_near, qkv_halves, gain_halves, out_sum = meet(attn_near, qkv_halves, gain_halves, out_sum)
    qkv_sum, gain_sum = swapped(qkv_halves, far), swapped(gain_halves, far)
    up_parts = reduce_y(up_sum, y)
    out_parts = reduce_y(out_sum, y)

    def finish_grad(back_attn, from_x, from_y, hid, scale_a, gain_a, d_mid):
        sc_a = scale_a.reshape(micro, 4 * toks, 1)[:, :toks]
        d_normed_a = scatter_sum(back_attn, (from_x, from_y))
        return d_mid + norm_back(d_normed_a, hid.astype(F32) * sc_a, gain_a, sc_a)

    input_grad = single(finish_grad, back_attn, *attn_near, hid, scale_a, gain_a, d_mid)
    input_grad = regroup(input_grad, block, c, True)
    input_grad, qkv_sum, gain_sum, up_parts, out_parts = meet(
        input_grad, qkv_sum, gain_sum, up_parts, out_parts
    )
    gain_parts = reduce_y(gain_sum, y)
    qkv_parts = reduce_y(qkv_sum, y)
    keep = add(*gain_parts)
    keep = keep + swap_x(keep)

    def cut(parts, lo, hi):
        return join((parts[0][:, lo:hi], parts[1][:, lo:hi]), y)

    return (
        block_out[:, None],
        input_grad[:, None],
        keep[0],
        keep[1],
        cut(qkv_parts, 0, q_cols),
        cut(qkv_parts, q_cols, q_cols + kv_cols),
        cut(qkv_parts, q_cols + kv_cols, qkv_cols),
        join(out_parts, y),
        join(gate_parts, y),
        join(up_parts, y),
        join(down_parts, y),
    )


def solution(mesh):
    n_dp, n_tensor = mesh.shape["dp"], mesh.shape["tensor"]
    grid = Mesh(mesh.devices.reshape(n_dp // 4, 2, 2, n_tensor), ("z", "y", "c", "x"))
    dp = ("z", "y", "c")
    token = P(None, dp, "x", None)
    weight = P(dp, "x")
    gain = P(dp)
    in_specs = (token, P(None, dp, None), gain, gain) + (weight,) * 7 + (token,)
    out_specs = (token, token, gain, gain) + (weight,) * 7
    return jax.shard_map(
        on_device, mesh=grid, in_specs=in_specs, out_specs=out_specs, check_vma=False
    )
```

```python
import jax
import jax.numpy as jnp
import numpy as np
from jax import lax
from jax.experimental import pallas as pl
from jax.experimental.pallas import tpu as pltpu
from jax.sharding import Mesh
from jax.sharding import PartitionSpec as P

HEAD_SIZE = 64
EPS = 1e-05
BF = jnp.bfloat16
F32 = jnp.float32


def swap_x(a):
    return lax.ppermute(a, "x", [(0, 1), (1, 0)])


def swap_y(a):
    return lax.ppermute(a, "y", [(0, 1), (1, 0)])


def swap_c(a):
    return lax.ppermute(a, "c", [(0, 1), (1, 0)])


def swap_z(a, bit):
    n = lax.axis_size("z")
    return lax.ppermute(a, "z", [(i, i ^ bit) for i in range(n)])


def far_bits():
    n = lax.axis_size("z")
    bits = []
    bit = n // 2
    while bit:
        bits.append(bit)
        bit //= 2
    return bits


def z_order():
    order = [0]
    for bit in far_bits():
        order = order + [r ^ bit for r in order]
    return order


def meet(*values):
    return lax.optimization_barrier(values)


def single(work, *args):
    shapes = jax.eval_shape(work, *args)
    return lax.cond(
        lax.axis_index("z") >= 0,
        work,
        lambda *_: jax.tree.map(lambda s: jnp.zeros(s.shape, s.dtype), shapes),
        *args,
    )


def gather_near(own):
    return own, swap_x(own), swap_y(own)


def diag_parts(near):
    half = near[1].shape[-1] // 2
    return near[1][..., :half], near[2][..., half:]


def gather_diag(parts):
    return swap_y(parts[0]), swap_x(parts[1])


def gather_join(near, diag):
    return jnp.concatenate(tuple(near) + (jnp.concatenate(diag, axis=-1),), axis=1)


def far_parts(part):
    m, rows, f = part.shape
    diag = part[:, 3 * rows // 4 :]
    return diag[..., : f // 2], diag[..., f // 2 :]


def scatter_far(parts):
    return swap_y(parts[0]), swap_x(parts[1])


def scatter_prep(part, far):
    m, rows, f = part.shape
    half = f // 2
    toks = rows // 4

    def kernel(x_ref, y_ref, low_ref, high_ref, to_x, to_y):
        to_x[0, :, :half] = add(x_ref[0, 0, :, :half], low_ref[0]).astype(BF)
        to_x[0, :, half:] = x_ref[0, 0, :, half:]
        to_y[0, :, :half] = y_ref[0, 0, :, :half]
        to_y[0, :, half:] = add(y_ref[0, 0, :, half:], high_ref[0]).astype(BF)

    part = part.reshape(m, 4, toks, f)
    small = pl.BlockSpec((1, toks, half), lambda i: (i, 0, 0))
    large = pl.BlockSpec((1, toks, f), lambda i: (i, 0, 0))
    return pl.pallas_call(
        kernel,
        out_shape=[jax.ShapeDtypeStruct((m, toks, f), BF)] * 2,
        grid=(m,),
        in_specs=[
            pl.BlockSpec((1, 1, toks, f), lambda i: (i, 1, 0, 0)),
            pl.BlockSpec((1, 1, toks, f), lambda i: (i, 2, 0, 0)),
            small,
            small,
        ],
        out_specs=[large, large],
        cost_estimate=pl.CostEstimate(flops=0, bytes_accessed=10 * m * toks * f, transcendentals=0),
    )(part, part, *far)


def scatter_near(to_x, to_y):
    return swap_x(to_x), swap_y(to_y)


def scatter_sum(part, near):
    rows = part.shape[1] // 4
    return part[:, :rows].astype(F32) + near[0].astype(F32) + near[1].astype(F32)


def column_part(a, index):
    width = a.shape[1] // 2
    return lax.dynamic_slice_in_dim(a, index * width, width, axis=1)


def pick(a, axis, index):
    return lax.dynamic_index_in_dim(a, index, axis, keepdims=False)


def z_first(*shards):
    held = jnp.stack(shards)[None]
    return held, swap_z(held, far_bits()[0])


def z_lead(pair):
    bits = far_bits()[1:-1]
    if not bits:
        return pair
    held = jnp.concatenate(pair, axis=0)
    for bit in bits:
        held = jnp.concatenate([held, swap_z(held, bit)], axis=0)
    half = held.shape[0] // 2
    return held[:half], held[half:]


def z_rest(pair):
    held = jnp.concatenate(z_lead(pair), axis=0)
    return held, swap_z(held, 1)


def both(pair):
    return jnp.concatenate(pair, axis=0)


def assemble(streams, z, y, extra=0, split=()):
    order = np.array(z_order() + [0], np.int32)
    n, _, rows, cols = streams[0][0].shape
    block = rows - extra
    last = np.arange(n + 1) == n
    where = jnp.where(jnp.asarray(last), y, jnp.asarray(order) ^ z)

    edges = (0,) + tuple(split) + (cols,)
    spans = list(zip(edges[:-1], edges[1:]))

    def kernel(where_ref, own, own_c, peer, peer_c, *more):
        yy = where_ref[n]
        for ref, at_c, at_y in ((own, 0, yy), (own_c, 1, yy), (peer, 0, 1 - yy), (peer_c, 1, 1 - yy)):
            if not extra:
                more[0][at_c, 0, at_y] = ref[0, 0]
                continue
            for out, (lo, hi) in zip(more, spans):
                out[at_c, 0, at_y] = ref[0, 0, :block, lo:hi]
            more[-1][at_c, 0, at_y] = ref[0, 0, block:, :128]

    out_shape = [jax.ShapeDtypeStruct((2, n, 2, block, hi - lo), BF) for lo, hi in spans]
    out_specs = [
        pl.BlockSpec((2, 1, 2, block, hi - lo), lambda i, at: (0, at[i], 0, 0, 0)) for lo, hi in spans
    ]
    if extra:
        out_shape.append(jax.ShapeDtypeStruct((2, n, 2, extra, 128), BF))
        out_specs.append(pl.BlockSpec((2, 1, 2, extra, 128), lambda i, at: (0, at[i], 0, 0, 0)))
    moved = 4 * n * rows * cols * 4
    return pl.pallas_call(
        kernel,
        out_shape=out_shape,
        grid_spec=pltpu.PrefetchScalarGridSpec(
            num_scalar_prefetch=1,
            grid=(n,),
            in_specs=[
                pl.BlockSpec((1, 1, rows, cols), lambda i, at, k=k: (i, k, 0, 0)) for _, k in streams
            ],
            out_specs=out_specs,
        ),
        cost_estimate=pl.CostEstimate(flops=0, bytes_accessed=moved, transcendentals=0),
    )(where, *(s for s, _ in streams))


def grad_half(index, left, right):
    nz = lax.axis_size("z")
    half = left.shape[1] // 2
    part = rows_rows(left[:, index * half : (index + 1) * half], right).astype(BF)
    return part.reshape(nz, 2, half // (2 * nz), right.shape[1])


def add(a, b):
    return a.astype(F32) + b.astype(F32)


def halve(pair, z, bit):
    n, _, block, cols = pair[0].shape
    pairs = [p.reshape(n // 2, 2, 2, block, cols) for p in pair]
    here = (z // bit) % 2
    keep = add(*(pick(p, 1, here) for p in pairs))
    send = add(*(pick(p, 1, 1 - here) for p in pairs))
    return keep, send.astype(pair[1].dtype)


def halve_near(pair, z):
    return halve(pair, z, 1)


def far_last():
    return far_bits()[0]


def far_steps(pair, z):
    for bit in far_bits()[1:-1][::-1]:
        pair = swapped(halve(pair, z, bit), bit)
    return pair


def halve_far(pair, z):
    return halve(far_steps(pair, z), z, far_last())


def swapped(halves, bit):
    return halves[0], swap_z(halves[1], bit)


def reduce_y(pair, y):
    keep, send = (add(*(pick(p[0], 0, at) for p in pair)) for at in (y, 1 - y))
    return keep, swap_y(send.astype(pair[1].dtype))


def side_by_side(low, high):
    return tuple(jnp.concatenate(p, axis=-1) for p in zip(low, high))


def columns(halves, lo, hi):
    return tuple(h[..., lo:hi] for h in halves)


def join(parts, y):
    mine, got = parts[0], parts[1].astype(F32)
    first = y == 0
    return jnp.concatenate([jnp.where(first, mine, got), jnp.where(first, got, mine)], axis=1)


def regroup(a, block, c, back=False):
    m, rows, width = a.shape
    half = width // 2
    count = half // block
    if block % 128:
        first = c == 0
        if back:
            own, other = (p.reshape(m, rows, count, block) for p in (a[..., :half], a[..., half:]))
            pair = jnp.stack([jnp.where(first, own, other), jnp.where(first, other, own)], axis=3)
            return pair.reshape(m, rows, width)
        pair = a.reshape(m, rows, count, 2, block)
        even, odd = pair[:, :, :, 0].reshape(m, rows, half), pair[:, :, :, 1].reshape(m, rows, half)
        return jnp.concatenate([jnp.where(first, even, odd), jnp.where(first, odd, even)], axis=-1)

    def kernel(core_ref, src, out):
        for core in range(2):

            @pl.when(core_ref[0] == core)
            def _():
                for i in range(count):
                    for r in range(2):
                        apart = pl.ds(r * half + i * block, block)
                        mixed = pl.ds((2 * i + (core ^ r)) * block, block)
                        if back:
                            out[:, mixed] = src[:, apart]
                        else:
                            out[:, apart] = src[:, mixed]

    step = 128
    total = m * rows
    out = pl.pallas_call(
        kernel,
        out_shape=jax.ShapeDtypeStruct((total, width), a.dtype),
        grid_spec=pltpu.PrefetchScalarGridSpec(
            num_scalar_prefetch=1,
            grid=(total // step,),
            in_specs=[pl.BlockSpec((step, width), lambda i, core: (i, 0))],
            out_specs=pl.BlockSpec((step, width), lambda i, core: (i, 0)),
        ),
        cost_estimate=pl.CostEstimate(
            flops=0, bytes_accessed=2 * total * width * a.dtype.itemsize, transcendentals=0
        ),
    )(c.reshape(1).astype(jnp.int32), a.reshape(total, width))
    return out.reshape(a.shape)


def reduce_z(grad, z, y):
    bit = 1
    for _ in far_bits():
        n, _, block, cols = grad.shape
        pairs = grad.reshape(n // 2, 2, 2, block, cols)
        here = (z // bit) % 2
        got = swap_z(pick(pairs, 1, 1 - here).astype(BF), bit)
        grad = pick(pairs, 1, here) + got.astype(F32)
        bit *= 2
    mine = pick(grad[0], 0, y)
    return mine, swap_y(pick(grad[0], 0, 1 - y).astype(BF)).astype(F32)


def rows_rows(left, right):
    return lax.dot_general(left, right, (((0,), (0,)), ((), ())), preferred_element_type=F32)


def cols_cols(left, right):
    return lax.dot_general(left, right, (((1,), (1,)), ((), ())), preferred_element_type=F32)


def turned(v, back=False):
    half = HEAD_SIZE // 2
    width = v.shape[-1]
    low = lax.broadcasted_iota(jnp.int32, v.shape, 1) % HEAD_SIZE < half
    up = pltpu.roll(v, width - half, 1)
    down = pltpu.roll(v, half, 1)
    return jnp.where(low, up, -down) if back else jnp.where(low, -up, down)


def head_probs(q, k, allowed):
    scores = jnp.where(allowed, cols_cols(k, q * BF(HEAD_SIZE ** (-0.5))), -1e30)
    expo = jnp.exp(scores - jnp.max(scores, axis=0, keepdims=True))
    return expo * (1.0 / jnp.sum(expo, axis=0, keepdims=True))


def wide(table, width):
    return jnp.concatenate([table] * (width // table.shape[1]), axis=1)


def attend(qkv, cos, sin, allowed, q_cols):
    groups, length, _ = cos.shape
    cols = qkv.shape[1]

    def kernel(qkv_ref, cos_ref, sin_ref, allowed_ref, q_out, kv_out, att_out):
        cos, sin = cos_ref[0], sin_ref[0]
        allowed = allowed_ref[0] > 0
        q_lin = qkv_ref[:, :q_cols]
        kv_lin = qkv_ref[:, q_cols:]
        q = (q_lin * wide(cos, q_cols) + turned(q_lin) * wide(sin, q_cols)).astype(BF)
        roped = kv_lin * cos + turned(kv_lin) * sin
        is_key = lax.broadcasted_iota(jnp.int32, kv_lin.shape, 1) < HEAD_SIZE
        kv = jnp.where(is_key, roped, kv_lin).astype(BF)
        q_out[...] = q
        kv_out[...] = kv
        k = kv[:, :HEAD_SIZE]
        v_t = kv_lin.T[HEAD_SIZE:].astype(BF)
        for pair in range(q_cols // (2 * HEAD_SIZE)):
            parts = []
            for h in (2 * pair, 2 * pair + 1):
                probs = head_probs(q[:, h * HEAD_SIZE : (h + 1) * HEAD_SIZE], k, allowed)
                parts.append(jnp.dot(v_t, probs.astype(BF), preferred_element_type=F32))
            at = pl.ds(pair * 2 * HEAD_SIZE, 2 * HEAD_SIZE)
            att_out[:, at] = jnp.concatenate(parts, axis=0).T.astype(BF)

    def rows(width):
        return pl.BlockSpec((length, width), lambda g: (g, 0))

    table = pl.BlockSpec((1, length, 2 * HEAD_SIZE), lambda g: (g, 0, 0))
    out = [jax.ShapeDtypeStruct((groups * length, w), BF) for w in (q_cols, cols - q_cols, q_cols)]
    return pl.pallas_call(
        kernel,
        out_shape=out,
        grid=(groups,),
        in_specs=[rows(cols), table, table, pl.BlockSpec((1, length, length), lambda g: (g, 0, 0))],
        out_specs=[rows(q_cols), rows(cols - q_cols), rows(q_cols)],
    )(qkv, cos, sin, allowed)


def attend_back(queries, keys_values, d_att, cos, sin, allowed):
    groups, length, _ = cos.shape
    q_cols, kv_cols = queries.shape[1], keys_values.shape[1]
    scale = HEAD_SIZE ** (-0.5)

    def kernel(q_ref, kv_ref, d_ref, cos_ref, sin_ref, allowed_ref, out):
        cos, sin = cos_ref[0], sin_ref[0]
        allowed = allowed_ref[0] > 0
        k, v = kv_ref[:, :HEAD_SIZE], kv_ref[:, HEAD_SIZE:]
        k_t = kv_ref[...].astype(F32).T[:HEAD_SIZE].astype(BF)
        d_k = jnp.zeros((length, HEAD_SIZE), F32)
        d_v = jnp.zeros((length, HEAD_SIZE), F32)
        for pair in range(q_cols // (2 * HEAD_SIZE)):
            parts = []
            for h in (2 * pair, 2 * pair + 1):
                at = slice(h * HEAD_SIZE, (h + 1) * HEAD_SIZE)
                q, d = q_ref[:, at], d_ref[:, at]
                probs = head_probs(q, k, allowed)
                d_probs = cols_cols(v, d)
                inner_sum = jnp.sum(probs * d_probs, axis=0, keepdims=True)
                d_scores = (probs * (d_probs - inner_sum)).astype(BF)
                parts.append(jnp.dot(k_t, d_scores, preferred_element_type=F32) * scale)
                d_k = d_k + jnp.dot(d_scores, q, preferred_element_type=F32)
                d_v = d_v + jnp.dot(probs.astype(BF), d, preferred_element_type=F32)
            d_q = jnp.concatenate(parts, axis=0).T
            d_q = d_q * cos + turned(d_q * sin, True)
            out[:, pl.ds(pair * 2 * HEAD_SIZE, 2 * HEAD_SIZE)] = d_q.astype(BF)
        d_kv = jnp.concatenate([d_k * scale, d_v], axis=1)
        is_key = lax.broadcasted_iota(jnp.int32, d_kv.shape, 1) < HEAD_SIZE
        roped = d_kv * cos + turned(d_kv * sin, True)
        out[:, q_cols:] = jnp.where(is_key, roped, d_kv).astype(BF)

    def rows(width):
        return pl.BlockSpec((length, width), lambda g: (g, 0))

    table = pl.BlockSpec((1, length, 2 * HEAD_SIZE), lambda g: (g, 0, 0))
    return pl.pallas_call(
        kernel,
        out_shape=jax.ShapeDtypeStruct((groups * length, q_cols + kv_cols), BF),
        grid=(groups,),
        in_specs=[
            rows(q_cols),
            rows(kv_cols),
            rows(q_cols),
            table,
            table,
            pl.BlockSpec((1, length, length), lambda g: (g, 0, 0)),
        ],
        out_specs=rows(q_cols + kv_cols),
    )(queries, keys_values, d_att, cos, sin, allowed)


def norm_back(d_normed, unit, gain, scale):
    d_unit = d_normed * gain
    return scale * (d_unit - unit * jnp.mean(d_unit * unit, axis=-1, keepdims=True))


def on_device(
    hidden_in,
    segment_ids,
    attn_gain,
    mlp_gain,
    w_query,
    key_weight,
    value_weight,
    w_out,
    w_gate,
    w_up,
    w_down,
    out_cotangent,
):
    z, y, c, x = (lax.axis_index(n) for n in ("z", "y", "c", "x"))
    nz = lax.axis_size("z")
    micro = hidden_in.shape[0]
    toks = hidden_in.shape[2]
    width = hidden_in.shape[3]
    block = w_query.shape[0]
    scale = HEAD_SIZE ** (-0.5)
    extra = 16

    def pack_attn(index):
        gains = jnp.stack([attn_gain, mlp_gain])
        body = jnp.concatenate(
            [
                column_part(w_query, index),
                column_part(key_weight, index),
                column_part(value_weight, index),
                column_part(w_out, index),
            ],
            axis=1,
        )
        gains = jnp.pad(gains, ((0, extra - 2), (0, body.shape[1] - block)))
        return jnp.concatenate([body, gains], axis=0)

    def pack_gu(index):
        return jnp.concatenate([column_part(w_gate, index), column_part(w_up, index)], axis=1)

    def pack_down(index):
        return column_part(w_down, index)

    q_cols = w_query.shape[1] // 2
    kv_cols = key_weight.shape[1] // 2
    qkv_cols = q_cols + 2 * kv_cols
    own_far = z_first(pack_attn(y))
    attn_theirs = swap_y(pack_attn(1 - y))
    other_ids = swap_y(segment_ids[:, 0])
    own_far, attn_theirs, other_ids, hid = meet(own_far, attn_theirs, other_ids, hidden_in[:, 0])
    peer_far = z_first(attn_theirs)
    attn_own = z_rest(own_far)
    hid = regroup(hid, block, c)
    hid_near = gather_near(hid)
    peer_far, attn_own, hid_near, hid_parts, gu_mine, gu_give = meet(
        peer_far, attn_own, hid_near, diag_parts(hid_near), pack_gu(y), pack_gu(1 - y)
    )
    attn_peer = z_rest(peer_far)
    gu_far = z_first(gu_mine)
    hid_diag = gather_diag(hid_parts)
    gu_theirs = swap_y(gu_give)
    attn_own = both(attn_own)
    cot = regroup(out_cotangent[:, 0], block, c)
    attn_peer, gu_far, hid_diag, gu_theirs, attn_own, cot, down_give = meet(
        attn_peer, gu_far, hid_diag, gu_theirs, attn_own, cot, pack_down(1 - y)
    )
    attn_own_c = swap_c(attn_own)
    attn_peer = both(attn_peer)
    attn_peer_c = swap_c(attn_peer)
    hid_all = gather_join(hid_near, hid_diag)
    gu_own = z_rest(gu_far)
    gu_peer = z_first(gu_theirs)
    cot_near = gather_near(cot)
    down_theirs = swap_y(down_give)
    attn_streams = ((attn_own, 0), (attn_own_c, 0), (attn_peer, 0), (attn_peer_c, 0))
    qkv_w, out_w, gains = assemble(attn_streams, z, y, extra, (qkv_cols,))
    qkv_w, out_w = qkv_w.reshape(width, -1), out_w.reshape(width, -1)
    gains = gains[:, :, :, :2, :block].astype(F32)
    gain_a = gains[:, :, :, 0].reshape(width)
    gain_m = gains[:, :, :, 1].reshape(width)

    length = 2 * toks
    groups = micro * 2
    ids = jnp.stack([segment_ids[:, 0], other_ids], axis=1).reshape(groups, length)
    ids = jnp.where(x == 0, ids, jnp.roll(ids, toks, axis=1))
    pos = (jnp.arange(length, dtype=jnp.int32) + toks * x) % length
    same = ids[:, :, None] == ids[:, None, :]
    allowed = jnp.logical_and(same, (pos[None, :] <= pos[:, None])[None])
    places = jnp.sum(allowed.astype(F32), axis=2) - 1.0
    freq = jnp.arange(HEAD_SIZE // 2, dtype=F32)
    inverse = 10000.0 ** (-2.0 * freq / HEAD_SIZE)
    angles = places[:, :, None] * inverse
    cos = jnp.concatenate([jnp.cos(angles)] * 4, axis=-1)
    sin = jnp.concatenate([jnp.sin(angles)] * 4, axis=-1)
    allowed = allowed.swapaxes(1, 2).astype(F32)

    rows = micro * 4 * toks
    heads = q_cols // HEAD_SIZE

    def attention(hid_all, gain_a, qkv_w, out_w, cos, sin, allowed):
        hid32 = hid_all.astype(F32).reshape(rows, width)
        scale_a = lax.rsqrt(jnp.mean(hid32 * hid32, axis=-1, keepdims=True) + EPS)
        normed_a = (hid32 * scale_a * gain_a).astype(BF)
        qkv = jnp.dot(normed_a, qkv_w, preferred_element_type=F32)
        queries, keys_values, attended = attend(qkv, cos, sin, allowed, q_cols)
        attn_part = cols_cols(attended, out_w).astype(BF).reshape(micro, 4 * toks, width)
        return scale_a, normed_a, queries, keys_values, attended, attn_part, far_parts(attn_part)

    scale_a, normed_a, queries, keys_values, attended, attn_part, attn_far = single(
        attention, hid_all, gain_a, qkv_w, out_w, cos, sin, allowed
    )
    attn_part, attn_far, gu_own, gu_peer, cot_near, down_theirs, down_mine = meet(
        attn_part, attn_far, gu_own, gu_peer, cot_near, down_theirs, pack_down(y)
    )
    attn_far = scatter_far(attn_far)
    gu_lead = z_lead(gu_peer)
    gu_low = swap_z(gu_lead[0], 1)
    ready, gu_low, gu_own = meet(scatter_prep(attn_part, attn_far), gu_low, gu_own)
    attn_near = scatter_near(*ready)
    gu_high = swap_z(gu_lead[1], 1)
    down_own = z_first(down_mine)
    gu_own = both(gu_own)
    gu_own_c = swap_c(gu_own)
    attn_near, gu_high, down_own, gu_own_c = meet(attn_near, gu_high, down_own, gu_own_c)
    gu_peer = jnp.concatenate([*gu_lead, gu_low, gu_high], axis=0)
    mid = hid.astype(F32) + scatter_sum(attn_part, attn_near)

    scale_m = lax.rsqrt(jnp.mean(mid * mid, axis=-1, keepdims=True) + EPS)
    unit_m = mid * scale_m
    normed_near = gather_near((unit_m * gain_m).astype(BF))
    gu_peer_c = swap_c(gu_peer)
    down_peer = z_first(down_theirs)
    down_own = z_rest(down_own)
    normed_near, normed_parts, gu_peer_c, down_peer, down_own = meet(
        normed_near, diag_parts(normed_near), gu_peer_c, down_peer, down_own
    )
    normed_diag = gather_diag(normed_parts)
    down_peer = z_rest(down_peer)
    gu_streams = ((gu_own, 0), (gu_own_c, 0), (gu_peer, 0), (gu_peer_c, 0))
    gu_w = assemble(gu_streams, z, y)[0].reshape(width, -1)
    down_own = both(down_own)
    down_own_c = swap_c(down_own)
    normed_diag, down_peer, gu_w, down_own_c, cot_parts = meet(
        normed_diag, down_peer, gu_w, down_own_c, diag_parts(cot_near)
    )
    normed_m, cot_parts = meet(gather_join(normed_near, normed_diag).reshape(rows, width), cot_parts)
    cot_diag = gather_diag(cot_parts)

    def feed(normed_m, gu_w):
        gu = jnp.dot(normed_m, gu_w, preferred_element_type=F32)
        ff = gu.shape[1] // 2
        return gu, (jax.nn.silu(gu[:, :ff]) * gu[:, ff:]).astype(BF)

    gu, inner = single(feed, normed_m, gu_w)
    inner, cot_diag, down_peer = meet(inner, cot_diag, down_peer)
    down_peer = both(down_peer)
    down_peer_c = swap_c(down_peer)
    cot_rows = gather_join(cot_near, cot_diag).reshape(rows, width)
    down_got = swap_c(grad_half(1, cot_rows, inner))
    down_streams = ((down_own, 0), (down_own_c, 0), (down_peer, 0), (down_peer_c, 0))
    down_w = assemble(down_streams, z, y)[0].reshape(width, -1)
    down_keep = single(lambda a, b: grad_half(0, a, b), cot_rows, inner)
    gu, down_w, down_halves = meet(gu, down_w, halve_near((down_keep, down_got), z))
    down_sum = swapped(down_halves, 1)

    def feed_back(gu, cot_rows, down_w, gu_w):
        d_inner = jnp.dot(cot_rows, down_w, preferred_element_type=F32)
        ff = gu.shape[1] // 2
        gate, up = gu[:, :ff], gu[:, ff:]
        sig = jax.nn.sigmoid(gate)
        d_gate = (d_inner * up * sig * (1.0 + gate * (1.0 - sig))).astype(BF)
        d_up = (d_inner * gate * sig).astype(BF)
        d_gu = jnp.concatenate([d_gate, d_up], axis=1)
        back = cols_cols(d_gu, gu_w).astype(BF)
        back = back.reshape(micro, 4 * toks, width)
        return d_gate, d_up, back, far_parts(back)

    ff = inner.shape[1]
    cols = (ff // 256 + 1) * 128 if ff % 256 else ff // 2
    far = far_bits()[0]
    d_gate, d_up, back_mlp, back_far = single(feed_back, gu, cot_rows, down_w, gu_w)
    ff = d_gate.shape[1]
    cols = (ff // 256 + 1) * 128 if ff % 256 else ff // 2
    far = far_bits()[0]
    back_mlp, back_far, d_gate, down_sum = meet(back_mlp, back_far, d_gate, down_sum)
    back_far = scatter_far(back_far)
    d_gate, down_low = meet(d_gate, halve_far(columns(down_sum, 0, cols), z))
    down_low = swapped(down_low, far)

    def gate_grads(normed_m, d_gate):
        return grad_half(1, normed_m, d_gate), grad_half(0, normed_m, d_gate)

    gate_send, gate_keep = single(gate_grads, normed_m, d_gate)
    down_high = halve_far(columns(down_sum, cols, ff), z)
    back_far, gate_send, gate_keep, down_low, down_high = meet(
        back_far, gate_send, gate_keep, down_low, down_high
    )
    gate_got = swap_c(gate_send)
    ready, gate_keep = meet(scatter_prep(back_mlp, back_far), gate_keep)
    back_near = scatter_near(*ready)
    down_high = swapped(down_high, far)
    gate_pair = gate_keep, gate_got
    d_up, gate_low, gate_high = meet(
        d_up, halve_near(columns(gate_pair, 0, cols), z), halve_near(columns(gate_pair, cols, ff), z)
    )
    gate_low = swapped(gate_low, 1)

    def up_grads(normed_m, d_up):
        return grad_half(1, normed_m, d_up), grad_half(0, normed_m, d_up)

    up_send, up_keep = single(up_grads, normed_m, d_up)
    back_near, down_low, gate_low, gate_high, down_high, up_send, up_keep = meet(
        back_near, down_low, gate_low, gate_high, down_high, up_send, up_keep
    )
    up_got = swap_c(up_send)

    def mid_back(back_mlp, from_x, from_y, unit_m, scale_m, gain_m, cot):
        d_normed_m = scatter_sum(back_mlp, (from_x, from_y))
        d_mid = cot.astype(F32) + norm_back(d_normed_m, unit_m, gain_m, scale_m)
        return d_mid, d_mid.astype(BF), jnp.sum(d_normed_m * unit_m, axis=(0, 1))

    d_mid, d_mid_low, gain_m_part = single(mid_back, back_mlp, *back_near, unit_m, scale_m, gain_m, cot)

    d_mid_low, up_got, inner = meet(d_mid_low, up_got, inner)
    d_mid_near = gather_near(d_mid_low)
    gate_high = swapped(gate_high, 1)
    gate_low = swapped(halve_far(gate_low, z), far)

    def mlp_out(inner, down_w):
        part = cols_cols(inner, down_w).astype(BF).reshape(micro, 4 * toks, width)
        return part, far_parts(part)

    mlp_part, mlp_far = single(mlp_out, inner, down_w)
    up_pair = up_keep, up_got
    up_halves = halve_near(up_pair, z)
    d_mid_near, d_mid_parts, gate_high, up_halves, gate_low, mlp_part = meet(
        d_mid_near, diag_parts(d_mid_near), gate_high, up_halves, gate_low, mlp_part
    )
    d_mid_diag = gather_diag(d_mid_parts)
    up_sum = swapped(up_halves, 1)
    mlp_far, d_mid_diag, gate_high, down_sum = meet(
        mlp_far, d_mid_diag, halve_far(gate_high, z), side_by_side(down_low, down_high)
    )
    d_mid_all = gather_join(d_mid_near, d_mid_diag).reshape(rows, width)
    mlp_far = scatter_far(mlp_far)
    gate_high = swapped(gate_high, far)
    down_parts = reduce_y(down_sum, y)

    def attention_back(d_mid_all, out_w, queries, keys_values, attended, cos, sin, allowed):
        d_att = jnp.dot(d_mid_all, out_w, preferred_element_type=F32).astype(BF)
        d_qkv = attend_back(queries, keys_values, d_att, cos, sin, allowed)
        return d_qkv, grad_half(1, d_mid_all, attended), grad_half(0, d_mid_all, attended)

    d_qkv, out_send, out_keep = single(
        attention_back, d_mid_all, out_w, queries, keys_values, attended, cos, sin, allowed
    )
    d_qkv, out_send, mlp_far, gate_high, up_sum, down_parts = meet(
        d_qkv, out_send, mlp_far, gate_high, up_sum, down_parts
    )
    out_got = swap_c(out_send)
    d_qkv, ready, up_halves = meet(d_qkv, scatter_prep(mlp_part, mlp_far), halve_far(up_sum, z))
    mlp_near = scatter_near(*ready)
    up_sum = swapped(up_halves, far)
    d_qkv, out_halves = meet(d_qkv, halve_near((out_keep, out_got), z))
    out_sum = swapped(out_halves, 1)
    gate_parts = reduce_y(side_by_side(gate_low, gate_high), y)

    def qkv_back(d_qkv, qkv_w, hid_all, scale_a, gain_m_part, normed_a):
        back = cols_cols(d_qkv, qkv_w)
        unit_a = hid_all.astype(F32).reshape(rows, width) * scale_a
        gain_rows = jnp.stack([jnp.sum(back * unit_a, axis=0), gain_m_part]).reshape(2, 2, nz, 2, block)
        gain_rows = gain_rows.transpose(1, 2, 3, 0, 4)
        back = back.astype(BF).reshape(micro, 4 * toks, width)
        grads = grad_half(1, normed_a, d_qkv), grad_half(0, normed_a, d_qkv)
        return back, far_parts(back), gain_rows[1], gain_rows[0], *grads

    back_attn, attn_far, gain_send, gain_keep, qkv_send, qkv_keep = single(
        qkv_back, d_qkv, qkv_w, hid_all, scale_a, gain_m_part, normed_a
    )
    back_attn, attn_far, qkv_send, gain_send, mlp_near, out_sum, up_sum, gate_parts = meet(
        back_attn, attn_far, qkv_send, gain_send, mlp_near, out_sum, up_sum, gate_parts
    )
    attn_far = scatter_far(attn_far)
    gain_got = swap_c(gain_send)
    qkv_got = swap_c(qkv_send)

    qkv_got, gain_got, out_sum = meet(qkv_got, gain_got, out_sum)

    def tail_halves(qkv_pair, gain_pair, out_pair):
        return halve(qkv_pair, z, 1), halve(gain_pair, z, 1), halve(out_pair, z, far_last())

    qkv_halves, gain_halves, out_halves = single(
        tail_halves, (qkv_keep, qkv_got), (gain_keep, gain_got), far_steps(out_sum, z)
    )
    attn_far, qkv_halves, gain_halves, out_halves = meet(attn_far, qkv_halves, gain_halves, out_halves)
    qkv_sum, gain_sum = swapped(qkv_halves, 1), swapped(gain_halves, 1)
    ready, mlp_near = meet(scatter_prep(back_attn, attn_far), mlp_near)
    attn_near = scatter_near(*ready)
    out_sum = swapped(out_halves, far)

    def finish_out(mid, mlp_part, mlp_near):
        return (mid + scatter_sum(mlp_part, mlp_near)).astype(BF)

    block_out = regroup(single(finish_out, mid, mlp_part, mlp_near), block, c, True)
    qkv_sum, gain_sum, block_out = meet(qkv_sum, gain_sum, block_out)

    def far_halves(*pairs):
        return [halve(p, z, far_last()) for p in pairs]

    qkv_halves, gain_halves = single(far_halves, far_steps(qkv_sum, z), far_steps(gain_sum, z))
    attn_near, qkv_halves, gain_halves, out_sum = meet(attn_near, qkv_halves, gain_halves, out_sum)
    qkv_sum, gain_sum = swapped(qkv_halves, far), swapped(gain_halves, far)
    up_parts = reduce_y(up_sum, y)
    out_parts = reduce_y(out_sum, y)

    def finish_grad(back_attn, from_x, from_y, hid, scale_a, gain_a, d_mid):
        sc_a = scale_a.reshape(micro, 4 * toks, 1)[:, :toks]
        d_normed_a = scatter_sum(back_attn, (from_x, from_y))
        return d_mid + norm_back(d_normed_a, hid.astype(F32) * sc_a, gain_a, sc_a)

    input_grad = single(finish_grad, back_attn, *attn_near, hid, scale_a, gain_a, d_mid)
    input_grad = regroup(input_grad, block, c, True)
    input_grad, qkv_sum, gain_sum, up_parts, out_parts = meet(
        input_grad, qkv_sum, gain_sum, up_parts, out_parts
    )
    gain_parts = reduce_y(gain_sum, y)
    qkv_parts = reduce_y(qkv_sum, y)
    keep = add(*gain_parts)
    keep = keep + swap_x(keep)

    def cut(parts, lo, hi):
        return join((parts[0][:, lo:hi], parts[1][:, lo:hi]), y)

    return (
        block_out[:, None],
        input_grad[:, None],
        keep[0],
        keep[1],
        cut(qkv_parts, 0, q_cols),
        cut(qkv_parts, q_cols, q_cols + kv_cols),
        cut(qkv_parts, q_cols + kv_cols, qkv_cols),
        join(out_parts, y),
        join(gate_parts, y),
        join(up_parts, y),
        join(down_parts, y),
    )


def solution(mesh):
    n_dp, n_tensor = mesh.shape["dp"], mesh.shape["tensor"]
    grid = Mesh(mesh.devices.reshape(n_dp // 4, 2, 2, n_tensor), ("z", "y", "c", "x"))
    dp = ("z", "y", "c")
    token = P(None, dp, "x", None)
    weight = P(dp, "x")
    gain = P(dp)
    in_specs = (token, P(None, dp, None), gain, gain) + (weight,) * 7 + (token,)
    out_specs = (token, token, gain, gain) + (weight,) * 7
    return jax.shard_map(
        on_device, mesh=grid, in_specs=in_specs, out_specs=out_specs, check_vma=False
    )
```

```python
import jax
import jax.numpy as jnp
import numpy as np
from jax import lax
from jax.experimental import pallas as pl
from jax.experimental.pallas import tpu as pltpu
from jax.sharding import Mesh
from jax.sharding import PartitionSpec as P

HEAD_SIZE = 64
EPS = 1e-05
BF = jnp.bfloat16
F32 = jnp.float32


def swap_x(a):
    return lax.ppermute(a, "x", [(0, 1), (1, 0)])


def swap_y(a):
    return lax.ppermute(a, "y", [(0, 1), (1, 0)])


def swap_c(a):
    return lax.ppermute(a, "c", [(0, 1), (1, 0)])


def swap_z(a, bit):
    n = lax.axis_size("z")
    return lax.ppermute(a, "z", [(i, i ^ bit) for i in range(n)])


def far_bits():
    n = lax.axis_size("z")
    bits = []
    bit = n // 2
    while bit:
        bits.append(bit)
        bit //= 2
    return bits


def z_order():
    order = [0]
    for bit in far_bits():
        order = order + [r ^ bit for r in order]
    return order


def meet(*values):
    return lax.optimization_barrier(values)


def single(work, *args):
    shapes = jax.eval_shape(work, *args)
    return lax.cond(
        lax.axis_index("z") >= 0,
        work,
        lambda *_: jax.tree.map(lambda s: jnp.zeros(s.shape, s.dtype), shapes),
        *args,
    )


def gather_near(own):
    return own, swap_x(own), swap_y(own)


def diag_parts(near):
    half = near[1].shape[-1] // 2
    return near[1][..., :half], near[2][..., half:]


def gather_diag(parts):
    return swap_y(parts[0]), swap_x(parts[1])


def gather_join(near, diag):
    return jnp.concatenate(tuple(near) + (jnp.concatenate(diag, axis=-1),), axis=1)


def far_parts(part):
    m, rows, f = part.shape
    diag = part[:, 3 * rows // 4 :]
    return diag[..., : f // 2], diag[..., f // 2 :]


def scatter_far(parts):
    return swap_y(parts[0]), swap_x(parts[1])


def scatter_prep(part, far):
    m, rows, f = part.shape
    half = f // 2
    toks = rows // 4

    def kernel(x_ref, y_ref, low_ref, high_ref, to_x, to_y):
        to_x[0, :, :half] = add(x_ref[0, 0, :, :half], low_ref[0]).astype(BF)
        to_x[0, :, half:] = x_ref[0, 0, :, half:]
        to_y[0, :, :half] = y_ref[0, 0, :, :half]
        to_y[0, :, half:] = add(y_ref[0, 0, :, half:], high_ref[0]).astype(BF)

    part = part.reshape(m, 4, toks, f)
    small = pl.BlockSpec((1, toks, half), lambda i: (i, 0, 0))
    large = pl.BlockSpec((1, toks, f), lambda i: (i, 0, 0))
    return pl.pallas_call(
        kernel,
        out_shape=[jax.ShapeDtypeStruct((m, toks, f), BF)] * 2,
        grid=(m,),
        in_specs=[
            pl.BlockSpec((1, 1, toks, f), lambda i: (i, 1, 0, 0)),
            pl.BlockSpec((1, 1, toks, f), lambda i: (i, 2, 0, 0)),
            small,
            small,
        ],
        out_specs=[large, large],
        cost_estimate=pl.CostEstimate(flops=0, bytes_accessed=10 * m * toks * f, transcendentals=0),
    )(part, part, *far)


def scatter_near(to_x, to_y):
    return swap_x(to_x), swap_y(to_y)


def scatter_sum(part, near):
    rows = part.shape[1] // 4
    return part[:, :rows].astype(F32) + near[0].astype(F32) + near[1].astype(F32)


def column_part(a, index):
    width = a.shape[1] // 2
    return lax.dynamic_slice_in_dim(a, index * width, width, axis=1)


def pick(a, axis, index):
    return lax.dynamic_index_in_dim(a, index, axis, keepdims=False)


def z_first(*shards):
    held = jnp.stack(shards)[None]
    return held, swap_z(held, far_bits()[0])


def z_lead(pair):
    bits = far_bits()[1:-1]
    if not bits:
        return pair
    held = jnp.concatenate(pair, axis=0)
    for bit in bits:
        held = jnp.concatenate([held, swap_z(held, bit)], axis=0)
    half = held.shape[0] // 2
    return held[:half], held[half:]


def z_rest(pair):
    held = jnp.concatenate(z_lead(pair), axis=0)
    return held, swap_z(held, 1)


def both(pair):
    return jnp.concatenate(pair, axis=0)


def assemble(streams, z, y, extra=0, split=()):
    order = np.array(z_order() + [0], np.int32)
    n, _, rows, cols = streams[0][0].shape
    block = rows - extra
    last = np.arange(n + 1) == n
    where = jnp.where(jnp.asarray(last), y, jnp.asarray(order) ^ z)

    edges = (0,) + tuple(split) + (cols,)
    spans = list(zip(edges[:-1], edges[1:]))

    def kernel(where_ref, own, own_c, peer, peer_c, *more):
        yy = where_ref[n]
        for ref, at_c, at_y in ((own, 0, yy), (own_c, 1, yy), (peer, 0, 1 - yy), (peer_c, 1, 1 - yy)):
            if not extra:
                more[0][at_c, 0, at_y] = ref[0, 0]
                continue
            for out, (lo, hi) in zip(more, spans):
                out[at_c, 0, at_y] = ref[0, 0, :block, lo:hi]
            more[-1][at_c, 0, at_y] = ref[0, 0, block:, :128]

    out_shape = [jax.ShapeDtypeStruct((2, n, 2, block, hi - lo), BF) for lo, hi in spans]
    out_specs = [
        pl.BlockSpec((2, 1, 2, block, hi - lo), lambda i, at: (0, at[i], 0, 0, 0)) for lo, hi in spans
    ]
    if extra:
        out_shape.append(jax.ShapeDtypeStruct((2, n, 2, extra, 128), BF))
        out_specs.append(pl.BlockSpec((2, 1, 2, extra, 128), lambda i, at: (0, at[i], 0, 0, 0)))
    moved = 4 * n * rows * cols * 4
    return pl.pallas_call(
        kernel,
        out_shape=out_shape,
        grid_spec=pltpu.PrefetchScalarGridSpec(
            num_scalar_prefetch=1,
            grid=(n,),
            in_specs=[
                pl.BlockSpec((1, 1, rows, cols), lambda i, at, k=k: (i, k, 0, 0)) for _, k in streams
            ],
            out_specs=out_specs,
        ),
        cost_estimate=pl.CostEstimate(flops=0, bytes_accessed=moved, transcendentals=0),
    )(where, *(s for s, _ in streams))


def grad_half(index, left, right):
    nz = lax.axis_size("z")
    half = left.shape[1] // 2
    part = rows_rows(left[:, index * half : (index + 1) * half], right).astype(BF)
    return part.reshape(nz, 2, half // (2 * nz), right.shape[1])


def add(a, b):
    return a.astype(F32) + b.astype(F32)


def halve(pair, z, bit):
    n, _, block, cols = pair[0].shape
    pairs = [p.reshape(n // 2, 2, 2, block, cols) for p in pair]
    here = (z // bit) % 2
    keep = add(*(pick(p, 1, here) for p in pairs))
    send = add(*(pick(p, 1, 1 - here) for p in pairs))
    return keep, send.astype(pair[1].dtype)


def halve_near(pair, z):
    return halve(pair, z, 1)


def far_last():
    return far_bits()[0]


def far_steps(pair, z):
    for bit in far_bits()[1:-1][::-1]:
        pair = swapped(halve(pair, z, bit), bit)
    return pair


def halve_far(pair, z):
    return halve(far_steps(pair, z), z, far_last())


def swapped(halves, bit):
    return halves[0], swap_z(halves[1], bit)


def reduce_y(pair, y):
    keep, send = (add(*(pick(p[0], 0, at) for p in pair)) for at in (y, 1 - y))
    return keep, swap_y(send.astype(pair[1].dtype))


def side_by_side(low, high):
    return tuple(jnp.concatenate(p, axis=-1) for p in zip(low, high))


def columns(halves, lo, hi):
    return tuple(h[..., lo:hi] for h in halves)


def join(parts, y):
    mine, got = parts[0], parts[1].astype(F32)
    first = y == 0
    return jnp.concatenate([jnp.where(first, mine, got), jnp.where(first, got, mine)], axis=1)


def regroup(a, block, c, back=False):
    m, rows, width = a.shape
    half = width // 2
    count = half // block
    if block % 128:
        first = c == 0
        if back:
            own, other = (p.reshape(m, rows, count, block) for p in (a[..., :half], a[..., half:]))
            pair = jnp.stack([jnp.where(first, own, other), jnp.where(first, other, own)], axis=3)
            return pair.reshape(m, rows, width)
        pair = a.reshape(m, rows, count, 2, block)
        even, odd = pair[:, :, :, 0].reshape(m, rows, half), pair[:, :, :, 1].reshape(m, rows, half)
        return jnp.concatenate([jnp.where(first, even, odd), jnp.where(first, odd, even)], axis=-1)

    def kernel(core_ref, src, out):
        for core in range(2):

            @pl.when(core_ref[0] == core)
            def _():
                for i in range(count):
                    for r in range(2):
                        apart = pl.ds(r * half + i * block, block)
                        mixed = pl.ds((2 * i + (core ^ r)) * block, block)
                        if back:
                            out[:, mixed] = src[:, apart]
                        else:
                            out[:, apart] = src[:, mixed]

    step = 128
    total = m * rows
    out = pl.pallas_call(
        kernel,
        out_shape=jax.ShapeDtypeStruct((total, width), a.dtype),
        grid_spec=pltpu.PrefetchScalarGridSpec(
            num_scalar_prefetch=1,
            grid=(total // step,),
            in_specs=[pl.BlockSpec((step, width), lambda i, core: (i, 0))],
            out_specs=pl.BlockSpec((step, width), lambda i, core: (i, 0)),
        ),
        cost_estimate=pl.CostEstimate(
            flops=0, bytes_accessed=2 * total * width * a.dtype.itemsize, transcendentals=0
        ),
    )(c.reshape(1).astype(jnp.int32), a.reshape(total, width))
    return out.reshape(a.shape)


def reduce_z(grad, z, y):
    bit = 1
    for _ in far_bits():
        n, _, block, cols = grad.shape
        pairs = grad.reshape(n // 2, 2, 2, block, cols)
        here = (z // bit) % 2
        got = swap_z(pick(pairs, 1, 1 - here).astype(BF), bit)
        grad = pick(pairs, 1, here) + got.astype(F32)
        bit *= 2
    mine = pick(grad[0], 0, y)
    return mine, swap_y(pick(grad[0], 0, 1 - y).astype(BF)).astype(F32)


def rows_rows(left, right):
    return lax.dot_general(left, right, (((0,), (0,)), ((), ())), preferred_element_type=F32)


def cols_cols(left, right):
    return lax.dot_general(left, right, (((1,), (1,)), ((), ())), preferred_element_type=F32)


def turned(v, back=False):
    half = HEAD_SIZE // 2
    width = v.shape[-1]
    low = lax.broadcasted_iota(jnp.int32, v.shape, 1) % HEAD_SIZE < half
    up = pltpu.roll(v, width - half, 1)
    down = pltpu.roll(v, half, 1)
    return jnp.where(low, up, -down) if back else jnp.where(low, -up, down)


def head_probs(q, k, allowed):
    scores = jnp.where(allowed, cols_cols(k, q * BF(HEAD_SIZE ** (-0.5))), -1e30)
    expo = jnp.exp(scores - jnp.max(scores, axis=0, keepdims=True))
    return expo * (1.0 / jnp.sum(expo, axis=0, keepdims=True))


def wide(table, width):
    return jnp.concatenate([table] * (width // table.shape[1]), axis=1)


def attend(qkv, cos, sin, allowed, q_cols):
    groups, length, _ = cos.shape
    cols = qkv.shape[1]

    def kernel(qkv_ref, cos_ref, sin_ref, allowed_ref, q_out, kv_out, att_out):
        cos, sin = cos_ref[0], sin_ref[0]
        allowed = allowed_ref[0] > 0
        q_lin = qkv_ref[:, :q_cols]
        kv_lin = qkv_ref[:, q_cols:]
        q = (q_lin * wide(cos, q_cols) + turned(q_lin) * wide(sin, q_cols)).astype(BF)
        roped = kv_lin * cos + turned(kv_lin) * sin
        is_key = lax.broadcasted_iota(jnp.int32, kv_lin.shape, 1) < HEAD_SIZE
        kv = jnp.where(is_key, roped, kv_lin).astype(BF)
        q_out[...] = q
        kv_out[...] = kv
        k = kv[:, :HEAD_SIZE]
        v_t = kv_lin.T[HEAD_SIZE:].astype(BF)
        for pair in range(q_cols // (2 * HEAD_SIZE)):
            parts = []
            for h in (2 * pair, 2 * pair + 1):
                probs = head_probs(q[:, h * HEAD_SIZE : (h + 1) * HEAD_SIZE], k, allowed)
                parts.append(jnp.dot(v_t, probs.astype(BF), preferred_element_type=F32))
            at = pl.ds(pair * 2 * HEAD_SIZE, 2 * HEAD_SIZE)
            att_out[:, at] = jnp.concatenate(parts, axis=0).T.astype(BF)

    def rows(width):
        return pl.BlockSpec((length, width), lambda g: (g, 0))

    table = pl.BlockSpec((1, length, 2 * HEAD_SIZE), lambda g: (g, 0, 0))
    out = [jax.ShapeDtypeStruct((groups * length, w), BF) for w in (q_cols, cols - q_cols, q_cols)]
    return pl.pallas_call(
        kernel,
        out_shape=out,
        grid=(groups,),
        in_specs=[rows(cols), table, table, pl.BlockSpec((1, length, length), lambda g: (g, 0, 0))],
        out_specs=[rows(q_cols), rows(cols - q_cols), rows(q_cols)],
    )(qkv, cos, sin, allowed)


def attend_back(queries, keys_values, d_att, cos, sin, allowed):
    groups, length, _ = cos.shape
    q_cols, kv_cols = queries.shape[1], keys_values.shape[1]
    scale = HEAD_SIZE ** (-0.5)

    def kernel(q_ref, kv_ref, d_ref, cos_ref, sin_ref, allowed_ref, out):
        cos, sin = cos_ref[0], sin_ref[0]
        allowed = allowed_ref[0] > 0
        k, v = kv_ref[:, :HEAD_SIZE], kv_ref[:, HEAD_SIZE:]
        k_t = kv_ref[...].astype(F32).T[:HEAD_SIZE].astype(BF)
        d_k = jnp.zeros((length, HEAD_SIZE), F32)
        d_v = jnp.zeros((length, HEAD_SIZE), F32)
        for pair in range(q_cols // (2 * HEAD_SIZE)):
            parts = []
            for h in (2 * pair, 2 * pair + 1):
                at = slice(h * HEAD_SIZE, (h + 1) * HEAD_SIZE)
                q, d = q_ref[:, at], d_ref[:, at]
                probs = head_probs(q, k, allowed)
                d_probs = cols_cols(v, d)
                inner_sum = jnp.sum(probs * d_probs, axis=0, keepdims=True)
                d_scores = (probs * (d_probs - inner_sum)).astype(BF)
                parts.append(jnp.dot(k_t, d_scores, preferred_element_type=F32) * scale)
                d_k = d_k + jnp.dot(d_scores, q, preferred_element_type=F32)
                d_v = d_v + jnp.dot(probs.astype(BF), d, preferred_element_type=F32)
            d_q = jnp.concatenate(parts, axis=0).T
            d_q = d_q * cos + turned(d_q * sin, True)
            out[:, pl.ds(pair * 2 * HEAD_SIZE, 2 * HEAD_SIZE)] = d_q.astype(BF)
        d_kv = jnp.concatenate([d_k * scale, d_v], axis=1)
        is_key = lax.broadcasted_iota(jnp.int32, d_kv.shape, 1) < HEAD_SIZE
        roped = d_kv * cos + turned(d_kv * sin, True)
        out[:, q_cols:] = jnp.where(is_key, roped, d_kv).astype(BF)

    def rows(width):
        return pl.BlockSpec((length, width), lambda g: (g, 0))

    table = pl.BlockSpec((1, length, 2 * HEAD_SIZE), lambda g: (g, 0, 0))
    return pl.pallas_call(
        kernel,
        out_shape=jax.ShapeDtypeStruct((groups * length, q_cols + kv_cols), BF),
        grid=(groups,),
        in_specs=[
            rows(q_cols),
            rows(kv_cols),
            rows(q_cols),
            table,
            table,
            pl.BlockSpec((1, length, length), lambda g: (g, 0, 0)),
        ],
        out_specs=rows(q_cols + kv_cols),
    )(queries, keys_values, d_att, cos, sin, allowed)


def norm_back(d_normed, unit, gain, scale):
    d_unit = d_normed * gain
    return scale * (d_unit - unit * jnp.mean(d_unit * unit, axis=-1, keepdims=True))


def on_device(
    hidden_in,
    segment_ids,
    attn_gain,
    mlp_gain,
    w_query,
    key_weight,
    value_weight,
    w_out,
    w_gate,
    w_up,
    w_down,
    out_cotangent,
):
    z, y, c, x = (lax.axis_index(n) for n in ("z", "y", "c", "x"))
    nz = lax.axis_size("z")
    micro = hidden_in.shape[0]
    toks = hidden_in.shape[2]
    width = hidden_in.shape[3]
    block = w_query.shape[0]
    scale = HEAD_SIZE ** (-0.5)
    extra = 16

    def pack_attn(index):
        gains = jnp.stack([attn_gain, mlp_gain])
        body = jnp.concatenate(
            [
                column_part(w_query, index),
                column_part(key_weight, index),
                column_part(value_weight, index),
                column_part(w_out, index),
            ],
            axis=1,
        )
        gains = jnp.pad(gains, ((0, extra - 2), (0, body.shape[1] - block)))
        return jnp.concatenate([body, gains], axis=0)

    def pack_gu(index):
        return jnp.concatenate([column_part(w_gate, index), column_part(w_up, index)], axis=1)

    def pack_down(index):
        return column_part(w_down, index)

    q_cols = w_query.shape[1] // 2
    kv_cols = key_weight.shape[1] // 2
    qkv_cols = q_cols + 2 * kv_cols
    own_far = z_first(pack_attn(y))
    attn_theirs = swap_y(pack_attn(1 - y))
    other_ids = swap_y(segment_ids[:, 0])
    own_far, attn_theirs, other_ids, hid = meet(own_far, attn_theirs, other_ids, hidden_in[:, 0])
    length = 2 * toks
    groups = micro * 2
    ids = jnp.stack([segment_ids[:, 0], other_ids], axis=1).reshape(groups, length)
    ids = jnp.where(x == 0, ids, jnp.roll(ids, toks, axis=1))
    pos = (jnp.arange(length, dtype=jnp.int32) + toks * x) % length
    same = ids[:, :, None] == ids[:, None, :]
    allowed = jnp.logical_and(same, (pos[None, :] <= pos[:, None])[None])
    places = jnp.sum(allowed.astype(F32), axis=2) - 1.0
    freq = jnp.arange(HEAD_SIZE // 2, dtype=F32)
    inverse = 10000.0 ** (-2.0 * freq / HEAD_SIZE)
    angles = places[:, :, None] * inverse
    cos = jnp.concatenate([jnp.cos(angles)] * 4, axis=-1)
    sin = jnp.concatenate([jnp.sin(angles)] * 4, axis=-1)
    allowed = allowed.swapaxes(1, 2).astype(F32)

    peer_far = z_first(attn_theirs)
    attn_own = z_rest(own_far)
    hid = regroup(hid, block, c)
    hid_near = gather_near(hid)
    peer_far, attn_own, hid_near, hid_parts, gu_mine, gu_give = meet(
        peer_far, attn_own, hid_near, diag_parts(hid_near), pack_gu(y), pack_gu(1 - y)
    )
    attn_peer = z_rest(peer_far)
    gu_far = z_first(gu_mine)
    hid_diag = gather_diag(hid_parts)
    gu_theirs = swap_y(gu_give)
    attn_own = both(attn_own)
    cot = regroup(out_cotangent[:, 0], block, c)
    attn_peer, gu_far, hid_diag, gu_theirs, attn_own, cot, down_give, cos, sin, allowed = meet(
        attn_peer, gu_far, hid_diag, gu_theirs, attn_own, cot, pack_down(1 - y), cos, sin, allowed
    )
    attn_own_c = swap_c(attn_own)
    attn_peer = both(attn_peer)
    attn_peer_c = swap_c(attn_peer)
    hid_all = gather_join(hid_near, hid_diag)
    gu_own = z_rest(gu_far)
    gu_peer = z_first(gu_theirs)
    cot_near = gather_near(cot)
    down_theirs = swap_y(down_give)
    attn_streams = ((attn_own, 0), (attn_own_c, 0), (attn_peer, 0), (attn_peer_c, 0))
    qkv_w, out_w, gains = assemble(attn_streams, z, y, extra, (qkv_cols,))
    qkv_w, out_w = qkv_w.reshape(width, -1), out_w.reshape(width, -1)
    gains = gains[:, :, :, :2, :block].astype(F32)
    gain_a = gains[:, :, :, 0].reshape(width)
    gain_m = gains[:, :, :, 1].reshape(width)

    rows = micro * 4 * toks
    heads = q_cols // HEAD_SIZE

    def attention(hid_all, gain_a, qkv_w, out_w, cos, sin, allowed):
        hid32 = hid_all.astype(F32).reshape(rows, width)
        scale_a = lax.rsqrt(jnp.mean(hid32 * hid32, axis=-1, keepdims=True) + EPS)
        normed_a = (hid32 * scale_a * gain_a).astype(BF)
        qkv = jnp.dot(normed_a, qkv_w, preferred_element_type=F32)
        queries, keys_values, attended = attend(qkv, cos, sin, allowed, q_cols)
        attn_part = cols_cols(attended, out_w).astype(BF).reshape(micro, 4 * toks, width)
        return scale_a, normed_a, queries, keys_values, attended, attn_part, far_parts(attn_part)

    scale_a, normed_a, queries, keys_values, attended, attn_part, attn_far = single(
        attention, hid_all, gain_a, qkv_w, out_w, cos, sin, allowed
    )
    attn_part, attn_far, gu_own, gu_peer, cot_near, down_theirs, down_mine = meet(
        attn_part, attn_far, gu_own, gu_peer, cot_near, down_theirs, pack_down(y)
    )
    attn_far = scatter_far(attn_far)
    gu_lead = z_lead(gu_peer)
    gu_low = swap_z(gu_lead[0], 1)
    ready, gu_low, gu_own = meet(scatter_prep(attn_part, attn_far), gu_low, gu_own)
    attn_near = scatter_near(*ready)
    gu_high = swap_z(gu_lead[1], 1)
    down_own = z_first(down_mine)
    gu_own = both(gu_own)
    gu_own_c = swap_c(gu_own)
    attn_near, gu_high, down_own, gu_own_c = meet(attn_near, gu_high, down_own, gu_own_c)
    gu_peer = jnp.concatenate([*gu_lead, gu_low, gu_high], axis=0)
    mid = hid.astype(F32) + scatter_sum(attn_part, attn_near)

    scale_m = lax.rsqrt(jnp.mean(mid * mid, axis=-1, keepdims=True) + EPS)
    unit_m = mid * scale_m
    normed_near = gather_near((unit_m * gain_m).astype(BF))
    gu_peer_c = swap_c(gu_peer)
    down_peer = z_first(down_theirs)
    down_own = z_rest(down_own)
    normed_near, normed_parts, gu_peer_c, down_peer, down_own = meet(
        normed_near, diag_parts(normed_near), gu_peer_c, down_peer, down_own
    )
    normed_diag = gather_diag(normed_parts)
    down_peer = z_rest(down_peer)
    gu_streams = ((gu_own, 0), (gu_own_c, 0), (gu_peer, 0), (gu_peer_c, 0))
    gu_w = assemble(gu_streams, z, y)[0].reshape(width, -1)
    down_own = both(down_own)
    down_own_c = swap_c(down_own)
    normed_diag, down_peer, gu_w, down_own_c, cot_parts = meet(
        normed_diag, down_peer, gu_w, down_own_c, diag_parts(cot_near)
    )
    normed_m, cot_parts = meet(gather_join(normed_near, normed_diag).reshape(rows, width), cot_parts)
    cot_diag = gather_diag(cot_parts)

    def feed(normed_m, gu_w):
        gu = jnp.dot(normed_m, gu_w, preferred_element_type=F32)
        ff = gu.shape[1] // 2
        return gu, (jax.nn.silu(gu[:, :ff]) * gu[:, ff:]).astype(BF)

    gu, inner = single(feed, normed_m, gu_w)
    inner, cot_diag, down_peer = meet(inner, cot_diag, down_peer)
    down_peer = both(down_peer)
    down_peer_c = swap_c(down_peer)
    cot_rows = gather_join(cot_near, cot_diag).reshape(rows, width)
    down_got = swap_c(grad_half(1, cot_rows, inner))
    down_streams = ((down_own, 0), (down_own_c, 0), (down_peer, 0), (down_peer_c, 0))
    down_w = assemble(down_streams, z, y)[0].reshape(width, -1)
    down_keep = single(lambda a, b: grad_half(0, a, b), cot_rows, inner)
    gu, down_w, down_halves = meet(gu, down_w, halve_near((down_keep, down_got), z))
    down_sum = swapped(down_halves, 1)

    def feed_back(gu, cot_rows, down_w, gu_w):
        d_inner = jnp.dot(cot_rows, down_w, preferred_element_type=F32)
        ff = gu.shape[1] // 2
        gate, up = gu[:, :ff], gu[:, ff:]
        sig = jax.nn.sigmoid(gate)
        d_gate = (d_inner * up * sig * (1.0 + gate * (1.0 - sig))).astype(BF)
        d_up = (d_inner * gate * sig).astype(BF)
        d_gu = jnp.concatenate([d_gate, d_up], axis=1)
        back = cols_cols(d_gu, gu_w).astype(BF)
        back = back.reshape(micro, 4 * toks, width)
        return d_gate, d_up, back, far_parts(back)

    ff = inner.shape[1]
    cols = (ff // 256 + 1) * 128 if ff % 256 else ff // 2
    far = far_bits()[0]
    d_gate, d_up, back_mlp, back_far = single(feed_back, gu, cot_rows, down_w, gu_w)
    ff = d_gate.shape[1]
    cols = (ff // 256 + 1) * 128 if ff % 256 else ff // 2
    far = far_bits()[0]
    back_mlp, back_far, d_gate, down_sum = meet(back_mlp, back_far, d_gate, down_sum)
    back_far = scatter_far(back_far)
    d_gate, down_low = meet(d_gate, halve_far(columns(down_sum, 0, ff - cols), z))
    down_low = swapped(down_low, far)

    def gate_grads(normed_m, d_gate):
        return grad_half(1, normed_m, d_gate), grad_half(0, normed_m, d_gate)

    gate_send, gate_keep = single(gate_grads, normed_m, d_gate)
    down_high = halve_far(columns(down_sum, ff - cols, ff), z)
    back_far, gate_send, gate_keep, down_low, down_high = meet(
        back_far, gate_send, gate_keep, down_low, down_high
    )
    gate_got = swap_c(gate_send)
    ready, gate_keep = meet(scatter_prep(back_mlp, back_far), gate_keep)
    back_near = scatter_near(*ready)
    gate_pair = gate_keep, gate_got
    d_up, gate_low, gate_pair = meet(d_up, halve_near(columns(gate_pair, 0, cols), z), gate_pair)
    gate_low = swapped(gate_low, 1)
    gate_high = halve_near(columns(gate_pair, cols, ff), z)

    def up_grads(normed_m, d_up):
        return grad_half(1, normed_m, d_up), grad_half(0, normed_m, d_up)

    up_send, up_keep = single(up_grads, normed_m, d_up)
    back_near, down_low, gate_low, gate_high, down_high, up_send, up_keep = meet(
        back_near, down_low, gate_low, gate_high, down_high, up_send, up_keep
    )
    up_got = swap_c(up_send)

    def mid_back(back_mlp, from_x, from_y, unit_m, scale_m, gain_m, cot):
        d_normed_m = scatter_sum(back_mlp, (from_x, from_y))
        d_mid = cot.astype(F32) + norm_back(d_normed_m, unit_m, gain_m, scale_m)
        return d_mid, d_mid.astype(BF), jnp.sum(d_normed_m * unit_m, axis=(0, 1))

    d_mid, d_mid_low, gain_m_part = single(mid_back, back_mlp, *back_near, unit_m, scale_m, gain_m, cot)

    d_mid_low, up_got, inner = meet(d_mid_low, up_got, inner)
    d_mid_near = gather_near(d_mid_low)
    gate_high = swapped(gate_high, 1)
    gate_low = far_steps(gate_low, z)
    gate_low = swapped(single(lambda *p: halve(p, z, far_last()), *gate_low), far)

    def mlp_out(inner, down_w):
        part = cols_cols(inner, down_w).astype(BF).reshape(micro, 4 * toks, width)
        return part, far_parts(part)

    mlp_part, mlp_far = single(mlp_out, inner, down_w)
    up_pair = up_keep, up_got
    up_halves = single(lambda *p: halve(p, z, 1), *up_pair)
    d_mid_near, d_mid_parts, gate_high, up_halves, gate_low, mlp_part = meet(
        d_mid_near, diag_parts(d_mid_near), gate_high, up_halves, gate_low, mlp_part
    )
    d_mid_diag = gather_diag(d_mid_parts)
    up_sum = swapped(up_halves, 1)
    mlp_far, d_mid_diag, gate_high, down_high = meet(mlp_far, d_mid_diag, halve_far(gate_high, z), down_high)
    d_mid_all = gather_join(d_mid_near, d_mid_diag).reshape(rows, width)
    mlp_far = scatter_far(mlp_far)
    gate_high = swapped(gate_high, far)
    down_high = swapped(down_high, far)

    def attention_back(d_mid_all, out_w, queries, keys_values, attended, cos, sin, allowed):
        d_att = jnp.dot(d_mid_all, out_w, preferred_element_type=F32).astype(BF)
        d_qkv = attend_back(queries, keys_values, d_att, cos, sin, allowed)
        return d_qkv, grad_half(1, d_mid_all, attended), grad_half(0, d_mid_all, attended)

    d_qkv, out_send, out_keep = single(
        attention_back, d_mid_all, out_w, queries, keys_values, attended, cos, sin, allowed
    )
    d_qkv, out_send, mlp_far, gate_high, up_sum, down_high = meet(
        d_qkv, out_send, mlp_far, gate_high, up_sum, down_high
    )
    out_got = swap_c(out_send)
    up_sum, ready = meet(up_sum, scatter_prep(mlp_part, mlp_far))
    mlp_near = scatter_near(*ready)
    d_qkv, up_halves = meet(d_qkv, halve_far(up_sum, z))
    up_sum = swapped(up_halves, far)
    d_qkv, out_halves = meet(d_qkv, halve_near((out_keep, out_got), z))
    out_sum = swapped(out_halves, 1)
    down_parts = reduce_y(side_by_side(down_low, down_high), y)

    def qkv_back(d_qkv, qkv_w, hid_all, scale_a, gain_m_part, normed_a):
        back = cols_cols(d_qkv, qkv_w)
        unit_a = hid_all.astype(F32).reshape(rows, width) * scale_a
        gain_rows = jnp.stack([jnp.sum(back * unit_a, axis=0), gain_m_part]).reshape(2, 2, nz, 2, block)
        gain_rows = gain_rows.transpose(1, 2, 3, 0, 4)
        back = back.astype(BF).reshape(micro, 4 * toks, width)
        grads = grad_half(1, normed_a, d_qkv), grad_half(0, normed_a, d_qkv)
        return back, far_parts(back), gain_rows[1], gain_rows[0], *grads

    back_attn, attn_far, gain_send, gain_keep, qkv_send, qkv_keep = single(
        qkv_back, d_qkv, qkv_w, hid_all, scale_a, gain_m_part, normed_a
    )
    back_attn, attn_far, qkv_send, gain_send, mlp_near, out_sum, up_sum, down_parts, gate_sum = meet(
        back_attn,
        attn_far,
        qkv_send,
        gain_send,
        mlp_near,
        out_sum,
        up_sum,
        down_parts,
        side_by_side(gate_low, gate_high),
    )
    attn_far = scatter_far(attn_far)
    gain_got = swap_c(gain_send)
    qkv_got = swap_c(qkv_send)

    qkv_got, gain_got, out_sum = meet(qkv_got, gain_got, out_sum)

    def tail_halves(qkv_pair, gain_pair, out_pair):
        return halve(qkv_pair, z, 1), halve(gain_pair, z, 1), halve(out_pair, z, far_last())

    qkv_halves, gain_halves, out_halves = single(
        tail_halves, (qkv_keep, qkv_got), (gain_keep, gain_got), far_steps(out_sum, z)
    )
    attn_far, qkv_halves, gain_halves, out_halves = meet(attn_far, qkv_halves, gain_halves, out_halves)
    qkv_sum, gain_sum = swapped(qkv_halves, 1), swapped(gain_halves, 1)
    ready, mlp_near = meet(scatter_prep(back_attn, attn_far), mlp_near)
    attn_near = scatter_near(*ready)
    out_sum = swapped(out_halves, far)

    def finish_out(mid, mlp_part, mlp_near):
        return (mid + scatter_sum(mlp_part, mlp_near)).astype(BF)

    block_out = regroup(single(finish_out, mid, mlp_part, mlp_near), block, c, True)
    qkv_sum, gain_sum, block_out = meet(qkv_sum, gain_sum, block_out)

    def far_halves(*pairs):
        return [halve(p, z, far_last()) for p in pairs]

    qkv_halves, gain_halves = single(far_halves, far_steps(qkv_sum, z), far_steps(gain_sum, z))
    attn_near, qkv_halves, gain_halves, out_sum = meet(attn_near, qkv_halves, gain_halves, out_sum)
    qkv_sum, gain_sum = swapped(qkv_halves, far), swapped(gain_halves, far)
    up_parts = reduce_y(up_sum, y)
    gate_parts = reduce_y(gate_sum, y)
    out_parts = reduce_y(out_sum, y)

    def finish_grad(back_attn, from_x, from_y, hid, scale_a, gain_a, d_mid):
        sc_a = scale_a.reshape(micro, 4 * toks, 1)[:, :toks]
        d_normed_a = scatter_sum(back_attn, (from_x, from_y))
        return d_mid + norm_back(d_normed_a, hid.astype(F32) * sc_a, gain_a, sc_a)

    input_grad = single(finish_grad, back_attn, *attn_near, hid, scale_a, gain_a, d_mid)
    input_grad = regroup(input_grad, block, c, True)
    input_grad, qkv_sum, gain_sum, up_parts, gate_parts, out_parts = meet(
        input_grad, qkv_sum, gain_sum, up_parts, gate_parts, out_parts
    )
    gain_parts = reduce_y(gain_sum, y)
    qkv_parts = reduce_y(qkv_sum, y)
    keep = add(*gain_parts)
    keep = keep + swap_x(keep)

    def cut(parts, lo, hi):
        return join((parts[0][:, lo:hi], parts[1][:, lo:hi]), y)

    return (
        block_out[:, None],
        input_grad[:, None],
        keep[0],
        keep[1],
        cut(qkv_parts, 0, q_cols),
        cut(qkv_parts, q_cols, q_cols + kv_cols),
        cut(qkv_parts, q_cols + kv_cols, qkv_cols),
        join(out_parts, y),
        join(gate_parts, y),
        join(up_parts, y),
        join(down_parts, y),
    )


def solution(mesh):
    n_dp, n_tensor = mesh.shape["dp"], mesh.shape["tensor"]
    grid = Mesh(mesh.devices.reshape(n_dp // 4, 2, 2, n_tensor), ("z", "y", "c", "x"))
    dp = ("z", "y", "c")
    token = P(None, dp, "x", None)
    weight = P(dp, "x")
    gain = P(dp)
    in_specs = (token, P(None, dp, None), gain, gain) + (weight,) * 7 + (token,)
    out_specs = (token, token, gain, gain) + (weight,) * 7
    return jax.shard_map(
        on_device, mesh=grid, in_specs=in_specs, out_specs=out_specs, check_vma=False
    )
```

```python
import jax
import jax.numpy as jnp
import numpy as np
from jax import lax
from jax.experimental import pallas as pl
from jax.experimental.pallas import tpu as pltpu
from jax.sharding import Mesh
from jax.sharding import PartitionSpec as P

HEAD_SIZE = 64
EPS = 1e-05
BF = jnp.bfloat16
F32 = jnp.float32


def swap_x(a):
    return lax.ppermute(a, "x", [(0, 1), (1, 0)])


def swap_y(a):
    return lax.ppermute(a, "y", [(0, 1), (1, 0)])


def swap_diagonal(a):
    return lax.ppermute(a, ("y", "x"), [(i, 3 - i) for i in range(4)])


def swap_c(a):
    return lax.ppermute(a, "c", [(0, 1), (1, 0)])


def swap_z(a, bit):
    n = lax.axis_size("z")
    return lax.ppermute(a, "z", [(i, i ^ bit) for i in range(n)])


def far_bits():
    n = lax.axis_size("z")
    bits = []
    bit = n // 2
    while bit:
        bits.append(bit)
        bit //= 2
    return bits


def z_order():
    order = [0]
    for bit in far_bits():
        order = order + [r ^ bit for r in order]
    return order


def meet(*values):
    return lax.optimization_barrier(values)


def single(work, *args):
    shapes = jax.eval_shape(work, *args)
    return lax.cond(
        lax.axis_index("z") >= 0,
        work,
        lambda *_: jax.tree.map(lambda s: jnp.zeros(s.shape, s.dtype), shapes),
        *args,
    )


def gather_near(own):
    return own, swap_x(own), swap_y(own)


def diag_parts(near):
    half = near[1].shape[-1] // 2
    return near[1][..., :half], near[2][..., half:]


def gather_diag(parts):
    return swap_y(parts[0]), swap_x(parts[1])


def gather_join(near, diag):
    return jnp.concatenate(tuple(near) + (jnp.concatenate(diag, axis=-1),), axis=1)


def far_parts(part):
    m, rows, f = part.shape
    diag = part[:, 3 * rows // 4 :]
    return diag[..., : f // 2], diag[..., f // 2 :]


def scatter_far(parts):
    return swap_y(parts[0]), swap_x(parts[1])


def scatter_prep(part, far):
    m, rows, f = part.shape
    half = f // 2
    toks = rows // 4

    def kernel(x_ref, y_ref, low_ref, high_ref, to_x, to_y):
        to_x[0, :, :half] = add(x_ref[0, 0, :, :half], low_ref[0]).astype(BF)
        to_x[0, :, half:] = x_ref[0, 0, :, half:]
        to_y[0, :, :half] = y_ref[0, 0, :, :half]
        to_y[0, :, half:] = add(y_ref[0, 0, :, half:], high_ref[0]).astype(BF)

    part = part.reshape(m, 4, toks, f)
    small = pl.BlockSpec((1, toks, half), lambda i: (i, 0, 0))
    large = pl.BlockSpec((1, toks, f), lambda i: (i, 0, 0))
    return pl.pallas_call(
        kernel,
        out_shape=[jax.ShapeDtypeStruct((m, toks, f), BF)] * 2,
        grid=(m,),
        in_specs=[
            pl.BlockSpec((1, 1, toks, f), lambda i: (i, 1, 0, 0)),
            pl.BlockSpec((1, 1, toks, f), lambda i: (i, 2, 0, 0)),
            small,
            small,
        ],
        out_specs=[large, large],
        cost_estimate=pl.CostEstimate(flops=0, bytes_accessed=10 * m * toks * f, transcendentals=0),
    )(part, part, *far)


def scatter_near(to_x, to_y):
    return swap_x(to_x), swap_y(to_y)


def scatter_sum(part, near):
    rows = part.shape[1] // 4
    return part[:, :rows].astype(F32) + near[0].astype(F32) + near[1].astype(F32)


def column_part(a, index):
    width = a.shape[1] // 2
    return lax.dynamic_slice_in_dim(a, index * width, width, axis=1)


def pick(a, axis, index):
    return lax.dynamic_index_in_dim(a, index, axis, keepdims=False)


def z_first(*shards):
    held = jnp.stack(shards)[None]
    return held, swap_z(held, far_bits()[0])


def z_lead(pair):
    bits = far_bits()[1:-1]
    if not bits:
        return pair
    held = jnp.concatenate(pair, axis=0)
    for bit in bits:
        held = jnp.concatenate([held, swap_z(held, bit)], axis=0)
    half = held.shape[0] // 2
    return held[:half], held[half:]


def z_rest(pair):
    held = jnp.concatenate(z_lead(pair), axis=0)
    return held, swap_z(held, 1)


def both(pair):
    return jnp.concatenate(pair, axis=0)


def assemble(streams, z, y, extra=0, split=()):
    order = np.array(z_order() + [0], np.int32)
    n, _, rows, cols = streams[0][0].shape
    block = rows - extra
    last = np.arange(n + 1) == n
    where = jnp.where(jnp.asarray(last), y, jnp.asarray(order) ^ z)

    edges = (0,) + tuple(split) + (cols,)
    spans = list(zip(edges[:-1], edges[1:]))

    def kernel(where_ref, own, own_c, peer, peer_c, *more):
        yy = where_ref[n]
        for ref, at_c, at_y in ((own, 0, yy), (own_c, 1, yy), (peer, 0, 1 - yy), (peer_c, 1, 1 - yy)):
            if not extra:
                more[0][at_c, 0, at_y] = ref[0, 0]
                continue
            for out, (lo, hi) in zip(more, spans):
                out[at_c, 0, at_y] = ref[0, 0, :block, lo:hi]
            more[-1][at_c, 0, at_y] = ref[0, 0, block:, :128]

    out_shape = [jax.ShapeDtypeStruct((2, n, 2, block, hi - lo), BF) for lo, hi in spans]
    out_specs = [
        pl.BlockSpec((2, 1, 2, block, hi - lo), lambda i, at: (0, at[i], 0, 0, 0)) for lo, hi in spans
    ]
    if extra:
        out_shape.append(jax.ShapeDtypeStruct((2, n, 2, extra, 128), BF))
        out_specs.append(pl.BlockSpec((2, 1, 2, extra, 128), lambda i, at: (0, at[i], 0, 0, 0)))
    moved = 4 * n * rows * cols * 4
    return pl.pallas_call(
        kernel,
        out_shape=out_shape,
        grid_spec=pltpu.PrefetchScalarGridSpec(
            num_scalar_prefetch=1,
            grid=(n,),
            in_specs=[
                pl.BlockSpec((1, 1, rows, cols), lambda i, at, k=k: (i, k, 0, 0)) for _, k in streams
            ],
            out_specs=out_specs,
        ),
        cost_estimate=pl.CostEstimate(flops=0, bytes_accessed=moved, transcendentals=0),
    )(where, *(s for s, _ in streams))


def grad_half(index, left, right):
    nz = lax.axis_size("z")
    half = left.shape[1] // 2
    part = rows_rows(left[:, index * half : (index + 1) * half], right).astype(BF)
    return part.reshape(nz, 2, half // (2 * nz), right.shape[1])


def add(a, b):
    return a.astype(F32) + b.astype(F32)


def halve(pair, z, bit):
    n, _, block, cols = pair[0].shape
    pairs = [p.reshape(n // 2, 2, 2, block, cols) for p in pair]
    here = (z // bit) % 2
    keep = add(*(pick(p, 1, here) for p in pairs))
    send = add(*(pick(p, 1, 1 - here) for p in pairs))
    return keep, send.astype(pair[1].dtype)


def halve_near(pair, z):
    return halve(pair, z, 1)


def far_last():
    return far_bits()[0]


def far_steps(pair, z):
    for bit in far_bits()[1:-1][::-1]:
        pair = swapped(halve(pair, z, bit), bit)
    return pair


def halve_far(pair, z):
    return halve(far_steps(pair, z), z, far_last())


def swapped(halves, bit):
    return halves[0], swap_z(halves[1], bit)


def reduce_y(pair, y):
    keep, send = (add(*(pick(p[0], 0, at) for p in pair)) for at in (y, 1 - y))
    return keep, swap_y(send.astype(pair[1].dtype))


def side_by_side(low, high):
    return tuple(jnp.concatenate(p, axis=-1) for p in zip(low, high))


def columns(halves, lo, hi):
    return tuple(h[..., lo:hi] for h in halves)


def join(parts, y):
    mine, got = parts[0], parts[1].astype(F32)
    first = y == 0
    return jnp.concatenate([jnp.where(first, mine, got), jnp.where(first, got, mine)], axis=1)


def regroup(a, block, c, back=False):
    m, rows, width = a.shape
    half = width // 2
    count = half // block
    if block % 128:
        first = c == 0
        if back:
            own, other = (p.reshape(m, rows, count, block) for p in (a[..., :half], a[..., half:]))
            pair = jnp.stack([jnp.where(first, own, other), jnp.where(first, other, own)], axis=3)
            return pair.reshape(m, rows, width)
        pair = a.reshape(m, rows, count, 2, block)
        even, odd = pair[:, :, :, 0].reshape(m, rows, half), pair[:, :, :, 1].reshape(m, rows, half)
        return jnp.concatenate([jnp.where(first, even, odd), jnp.where(first, odd, even)], axis=-1)

    def kernel(core_ref, src, out):
        for core in range(2):

            @pl.when(core_ref[0] == core)
            def _():
                for i in range(count):
                    for r in range(2):
                        apart = pl.ds(r * half + i * block, block)
                        mixed = pl.ds((2 * i + (core ^ r)) * block, block)
                        if back:
                            out[:, mixed] = src[:, apart]
                        else:
                            out[:, apart] = src[:, mixed]

    step = 128
    total = m * rows
    out = pl.pallas_call(
        kernel,
        out_shape=jax.ShapeDtypeStruct((total, width), a.dtype),
        grid_spec=pltpu.PrefetchScalarGridSpec(
            num_scalar_prefetch=1,
            grid=(total // step,),
            in_specs=[pl.BlockSpec((step, width), lambda i, core: (i, 0))],
            out_specs=pl.BlockSpec((step, width), lambda i, core: (i, 0)),
        ),
        cost_estimate=pl.CostEstimate(
            flops=0, bytes_accessed=2 * total * width * a.dtype.itemsize, transcendentals=0
        ),
    )(c.reshape(1).astype(jnp.int32), a.reshape(total, width))
    return out.reshape(a.shape)


def reduce_z(grad, z, y):
    bit = 1
    for _ in far_bits():
        n, _, block, cols = grad.shape
        pairs = grad.reshape(n // 2, 2, 2, block, cols)
        here = (z // bit) % 2
        got = swap_z(pick(pairs, 1, 1 - here).astype(BF), bit)
        grad = pick(pairs, 1, here) + got.astype(F32)
        bit *= 2
    mine = pick(grad[0], 0, y)
    return mine, swap_y(pick(grad[0], 0, 1 - y).astype(BF)).astype(F32)


def rows_rows(left, right):
    return lax.dot_general(left, right, (((0,), (0,)), ((), ())), preferred_element_type=F32)


def cols_cols(left, right):
    return lax.dot_general(left, right, (((1,), (1,)), ((), ())), preferred_element_type=F32)


def turned(v, back=False):
    half = HEAD_SIZE // 2
    width = v.shape[-1]
    low = lax.broadcasted_iota(jnp.int32, v.shape, 1) % HEAD_SIZE < half
    up = pltpu.roll(v, width - half, 1)
    down = pltpu.roll(v, half, 1)
    return jnp.where(low, up, -down) if back else jnp.where(low, -up, down)


def head_probs(q, k, allowed):
    scores = jnp.where(allowed, cols_cols(k, q * BF(HEAD_SIZE ** (-0.5))), -1e30)
    expo = jnp.exp(scores - jnp.max(scores, axis=0, keepdims=True))
    return expo * (1.0 / jnp.sum(expo, axis=0, keepdims=True))


def wide(table, width):
    return jnp.concatenate([table] * (width // table.shape[1]), axis=1)


def attend(qkv, cos, sin, allowed, q_cols):
    groups, length, _ = cos.shape
    cols = qkv.shape[1]

    def kernel(qkv_ref, cos_ref, sin_ref, allowed_ref, q_out, kv_out, att_out):
        cos, sin = cos_ref[0], sin_ref[0]
        allowed = allowed_ref[0] > 0
        q_lin = qkv_ref[:, :q_cols]
        kv_lin = qkv_ref[:, q_cols:]
        q = (q_lin * wide(cos, q_cols) + turned(q_lin) * wide(sin, q_cols)).astype(BF)
        roped = kv_lin * cos + turned(kv_lin) * sin
        is_key = lax.broadcasted_iota(jnp.int32, kv_lin.shape, 1) < HEAD_SIZE
        kv = jnp.where(is_key, roped, kv_lin).astype(BF)
        q_out[...] = q
        kv_out[...] = kv
        k = kv[:, :HEAD_SIZE]
        v_t = kv_lin.T[HEAD_SIZE:].astype(BF)
        for pair in range(q_cols // (2 * HEAD_SIZE)):
            parts = []
            for h in (2 * pair, 2 * pair + 1):
                probs = head_probs(q[:, h * HEAD_SIZE : (h + 1) * HEAD_SIZE], k, allowed)
                parts.append(jnp.dot(v_t, probs.astype(BF), preferred_element_type=F32))
            at = pl.ds(pair * 2 * HEAD_SIZE, 2 * HEAD_SIZE)
            att_out[:, at] = jnp.concatenate(parts, axis=0).T.astype(BF)

    def rows(width):
        return pl.BlockSpec((length, width), lambda g: (g, 0))

    table = pl.BlockSpec((1, length, 2 * HEAD_SIZE), lambda g: (g, 0, 0))
    out = [jax.ShapeDtypeStruct((groups * length, w), BF) for w in (q_cols, cols - q_cols, q_cols)]
    return pl.pallas_call(
        kernel,
        out_shape=out,
        grid=(groups,),
        in_specs=[rows(cols), table, table, pl.BlockSpec((1, length, length), lambda g: (g, 0, 0))],
        out_specs=[rows(q_cols), rows(cols - q_cols), rows(q_cols)],
    )(qkv, cos, sin, allowed)


def attend_back(queries, keys_values, d_att, cos, sin, allowed):
    groups, length, _ = cos.shape
    q_cols, kv_cols = queries.shape[1], keys_values.shape[1]
    scale = HEAD_SIZE ** (-0.5)

    def kernel(q_ref, kv_ref, d_ref, cos_ref, sin_ref, allowed_ref, out):
        cos, sin = cos_ref[0], sin_ref[0]
        allowed = allowed_ref[0] > 0
        k, v = kv_ref[:, :HEAD_SIZE], kv_ref[:, HEAD_SIZE:]
        k_t = kv_ref[...].astype(F32).T[:HEAD_SIZE].astype(BF)
        d_k = jnp.zeros((length, HEAD_SIZE), F32)
        d_v = jnp.zeros((length, HEAD_SIZE), F32)
        for pair in range(q_cols // (2 * HEAD_SIZE)):
            parts = []
            for h in (2 * pair, 2 * pair + 1):
                at = slice(h * HEAD_SIZE, (h + 1) * HEAD_SIZE)
                q, d = q_ref[:, at], d_ref[:, at]
                probs = head_probs(q, k, allowed)
                d_probs = cols_cols(v, d)
                inner_sum = jnp.sum(probs * d_probs, axis=0, keepdims=True)
                d_scores = (probs * (d_probs - inner_sum)).astype(BF)
                parts.append(jnp.dot(k_t, d_scores, preferred_element_type=F32) * scale)
                d_k = d_k + jnp.dot(d_scores, q, preferred_element_type=F32)
                d_v = d_v + jnp.dot(probs.astype(BF), d, preferred_element_type=F32)
            d_q = jnp.concatenate(parts, axis=0).T
            d_q = d_q * cos + turned(d_q * sin, True)
            out[:, pl.ds(pair * 2 * HEAD_SIZE, 2 * HEAD_SIZE)] = d_q.astype(BF)
        d_kv = jnp.concatenate([d_k * scale, d_v], axis=1)
        is_key = lax.broadcasted_iota(jnp.int32, d_kv.shape, 1) < HEAD_SIZE
        roped = d_kv * cos + turned(d_kv * sin, True)
        out[:, q_cols:] = jnp.where(is_key, roped, d_kv).astype(BF)

    def rows(width):
        return pl.BlockSpec((length, width), lambda g: (g, 0))

    table = pl.BlockSpec((1, length, 2 * HEAD_SIZE), lambda g: (g, 0, 0))
    return pl.pallas_call(
        kernel,
        out_shape=jax.ShapeDtypeStruct((groups * length, q_cols + kv_cols), BF),
        grid=(groups,),
        in_specs=[
            rows(q_cols),
            rows(kv_cols),
            rows(q_cols),
            table,
            table,
            pl.BlockSpec((1, length, length), lambda g: (g, 0, 0)),
        ],
        out_specs=rows(q_cols + kv_cols),
    )(queries, keys_values, d_att, cos, sin, allowed)


def norm_back(d_normed, unit, gain, scale):
    d_unit = d_normed * gain
    return scale * (d_unit - unit * jnp.mean(d_unit * unit, axis=-1, keepdims=True))


def on_device(
    hidden_in,
    segment_ids,
    attn_gain,
    mlp_gain,
    w_query,
    key_weight,
    value_weight,
    w_out,
    w_gate,
    w_up,
    w_down,
    out_cotangent,
):
    z, y, c, x = (lax.axis_index(n) for n in ("z", "y", "c", "x"))
    nz = lax.axis_size("z")
    micro = hidden_in.shape[0]
    toks = hidden_in.shape[2]
    width = hidden_in.shape[3]
    block = w_query.shape[0]
    scale = HEAD_SIZE ** (-0.5)
    extra = 16

    def pack_attn(index):
        gains = jnp.stack([attn_gain, mlp_gain])
        body = jnp.concatenate(
            [
                column_part(w_query, index),
                column_part(key_weight, index),
                column_part(value_weight, index),
                column_part(w_out, index),
            ],
            axis=1,
        )
        gains = jnp.pad(gains, ((0, extra - 2), (0, body.shape[1] - block)))
        return jnp.concatenate([body, gains], axis=0)

    def pack_gu(index):
        return jnp.concatenate([column_part(w_gate, index), column_part(w_up, index)], axis=1)

    def pack_down(index):
        return column_part(w_down, index)

    q_cols = w_query.shape[1] // 2
    kv_cols = key_weight.shape[1] // 2
    qkv_cols = q_cols + 2 * kv_cols
    own_far = z_first(pack_attn(y))
    attn_theirs = swap_y(pack_attn(1 - y))
    other_ids = swap_y(segment_ids[:, 0])
    own_far, attn_theirs, other_ids, hid = meet(own_far, attn_theirs, other_ids, hidden_in[:, 0])
    length = 2 * toks
    groups = micro * 2
    ids = jnp.stack([segment_ids[:, 0], other_ids], axis=1).reshape(groups, length)
    ids = jnp.where(x == 0, ids, jnp.roll(ids, toks, axis=1))
    pos = (jnp.arange(length, dtype=jnp.int32) + toks * x) % length
    same = ids[:, :, None] == ids[:, None, :]
    allowed = jnp.logical_and(same, (pos[None, :] <= pos[:, None])[None])
    places = jnp.sum(allowed.astype(F32), axis=2) - 1.0
    freq = jnp.arange(HEAD_SIZE // 2, dtype=F32)
    inverse = 10000.0 ** (-2.0 * freq / HEAD_SIZE)
    angles = places[:, :, None] * inverse
    cos = jnp.concatenate([jnp.cos(angles)] * 4, axis=-1)
    sin = jnp.concatenate([jnp.sin(angles)] * 4, axis=-1)
    allowed = allowed.swapaxes(1, 2).astype(F32)

    peer_far = z_first(attn_theirs)
    attn_own = z_rest(own_far)
    hid = regroup(hid, block, c)
    hid_near = gather_near(hid)
    peer_far, attn_own, hid_near, hid_parts, gu_mine, gu_give = meet(
        peer_far, attn_own, hid_near, diag_parts(hid_near), pack_gu(y), pack_gu(1 - y)
    )
    attn_peer = z_rest(peer_far)
    gu_far = z_first(gu_mine)
    hid_diag = gather_diag(hid_parts)
    gu_theirs = swap_y(gu_give)
    attn_own = both(attn_own)
    cot = regroup(out_cotangent[:, 0], block, c)
    attn_peer, gu_far, hid_diag, gu_theirs, attn_own, cot, down_give, cos, sin, allowed = meet(
        attn_peer, gu_far, hid_diag, gu_theirs, attn_own, cot, pack_down(1 - y), cos, sin, allowed
    )
    attn_own_c = swap_c(attn_own)
    attn_peer = both(attn_peer)
    attn_peer_c = swap_c(attn_peer)
    hid_all = gather_join(hid_near, hid_diag)
    gu_own = z_rest(gu_far)
    gu_peer = z_first(gu_theirs)
    cot_near = gather_near(cot)
    down_theirs = swap_y(down_give)
    attn_streams = ((attn_own, 0), (attn_own_c, 0), (attn_peer, 0), (attn_peer_c, 0))
    qkv_w, out_w, gains = assemble(attn_streams, z, y, extra, (qkv_cols,))
    qkv_w, out_w = qkv_w.reshape(width, -1), out_w.reshape(width, -1)
    gains = gains[:, :, :, :2, :block].astype(F32)
    gain_a = gains[:, :, :, 0].reshape(width)
    gain_m = gains[:, :, :, 1].reshape(width)

    rows = micro * 4 * toks
    heads = q_cols // HEAD_SIZE

    def attention(hid_all, gain_a, qkv_w, out_w, cos, sin, allowed):
        hid32 = hid_all.astype(F32).reshape(rows, width)
        scale_a = lax.rsqrt(jnp.mean(hid32 * hid32, axis=-1, keepdims=True) + EPS)
        normed_a = (hid32 * scale_a * gain_a).astype(BF)
        qkv = jnp.dot(normed_a, qkv_w, preferred_element_type=F32)
        queries, keys_values, attended = attend(qkv, cos, sin, allowed, q_cols)
        attn_part = cols_cols(attended, out_w).astype(BF).reshape(micro, 4 * toks, width)
        return scale_a, normed_a, queries, keys_values, attended, attn_part, far_parts(attn_part)

    scale_a, normed_a, queries, keys_values, attended, attn_part, attn_far = single(
        attention, hid_all, gain_a, qkv_w, out_w, cos, sin, allowed
    )
    attn_part, attn_far, gu_own, gu_peer, cot_near, down_theirs, down_mine = meet(
        attn_part, attn_far, gu_own, gu_peer, cot_near, down_theirs, pack_down(y)
    )
    attn_far = scatter_far(attn_far)
    gu_lead = z_lead(gu_peer)
    gu_low = swap_z(gu_lead[0], 1)
    ready, gu_low, gu_own = meet(scatter_prep(attn_part, attn_far), gu_low, gu_own)
    attn_near = scatter_near(*ready)
    gu_high = swap_z(gu_lead[1], 1)
    down_own = z_first(down_mine)
    gu_own = both(gu_own)
    gu_own_c = swap_c(gu_own)
    attn_near, gu_high, down_own, gu_own_c = meet(attn_near, gu_high, down_own, gu_own_c)
    gu_peer = jnp.concatenate([*gu_lead, gu_low, gu_high], axis=0)
    mid = hid.astype(F32) + scatter_sum(attn_part, attn_near)

    scale_m = lax.rsqrt(jnp.mean(mid * mid, axis=-1, keepdims=True) + EPS)
    unit_m = mid * scale_m
    normed_near = gather_near((unit_m * gain_m).astype(BF))
    gu_peer_c = swap_c(gu_peer)
    down_peer = z_first(down_theirs)
    down_own = z_rest(down_own)
    normed_near, normed_parts, gu_peer_c, down_peer, down_own = meet(
        normed_near, diag_parts(normed_near), gu_peer_c, down_peer, down_own
    )
    normed_diag = gather_diag(normed_parts)
    down_peer = z_rest(down_peer)
    gu_streams = ((gu_own, 0), (gu_own_c, 0), (gu_peer, 0), (gu_peer_c, 0))
    gu_w = assemble(gu_streams, z, y)[0].reshape(width, -1)
    down_own = both(down_own)
    down_own_c = swap_c(down_own)
    normed_diag, down_peer, gu_w, down_own_c, cot_parts = meet(
        normed_diag, down_peer, gu_w, down_own_c, diag_parts(cot_near)
    )
    normed_m, cot_parts = meet(gather_join(normed_near, normed_diag).reshape(rows, width), cot_parts)
    cot_diag = gather_diag(cot_parts)

    def feed(normed_m, gu_w):
        gu = jnp.dot(normed_m, gu_w, preferred_element_type=F32)
        ff = gu.shape[1] // 2
        return gu, (jax.nn.silu(gu[:, :ff]) * gu[:, ff:]).astype(BF)

    gu, inner = single(feed, normed_m, gu_w)
    inner, cot_diag, down_peer = meet(inner, cot_diag, down_peer)
    down_peer = both(down_peer)
    down_peer_c = swap_c(down_peer)
    cot_rows = gather_join(cot_near, cot_diag).reshape(rows, width)
    down_got = swap_c(grad_half(1, cot_rows, inner))
    down_streams = ((down_own, 0), (down_own_c, 0), (down_peer, 0), (down_peer_c, 0))
    down_w = assemble(down_streams, z, y)[0].reshape(width, -1)
    down_keep = single(lambda a, b: grad_half(0, a, b), cot_rows, inner)
    gu, down_w, down_halves = meet(gu, down_w, halve_near((down_keep, down_got), z))
    down_sum = swapped(down_halves, 1)

    def feed_back(gu, cot_rows, down_w, gu_w):
        d_inner = jnp.dot(cot_rows, down_w, preferred_element_type=F32)
        ff = gu.shape[1] // 2
        gate, up = gu[:, :ff], gu[:, ff:]
        sig = jax.nn.sigmoid(gate)
        d_gate = (d_inner * up * sig * (1.0 + gate * (1.0 - sig))).astype(BF)
        d_up = (d_inner * gate * sig).astype(BF)
        d_gu = jnp.concatenate([d_gate, d_up], axis=1)
        back = cols_cols(d_gu, gu_w).astype(BF)
        back = back.reshape(micro, 4 * toks, width)
        return d_gate, d_up, back, far_parts(back)

    ff = inner.shape[1]
    cols = (ff // 256 + 1) * 128 if ff % 256 else ff // 2
    far = far_bits()[0]
    d_gate, d_up, back_mlp, back_far = single(feed_back, gu, cot_rows, down_w, gu_w)
    ff = d_gate.shape[1]
    cols = (ff // 256 + 1) * 128 if ff % 256 else ff // 2
    far = far_bits()[0]
    back_mlp, back_far, d_gate, down_sum = meet(back_mlp, back_far, d_gate, down_sum)
    back_far = scatter_far(back_far)
    d_gate, down_low = meet(d_gate, halve_far(columns(down_sum, 0, ff - cols), z))
    down_low = swapped(down_low, far)

    def gate_grads(normed_m, d_gate):
        return grad_half(1, normed_m, d_gate), grad_half(0, normed_m, d_gate)

    gate_send, gate_keep = single(gate_grads, normed_m, d_gate)
    down_high = halve_far(columns(down_sum, ff - cols, ff), z)
    back_far, gate_send, gate_keep, down_low, down_high = meet(
        back_far, gate_send, gate_keep, down_low, down_high
    )
    gate_got = swap_c(gate_send)
    ready, gate_keep = meet(scatter_prep(back_mlp, back_far), gate_keep)
    back_near = scatter_near(*ready)
    gate_pair = gate_keep, gate_got
    d_up, gate_low, gate_pair = meet(d_up, halve_near(columns(gate_pair, 0, cols), z), gate_pair)
    gate_low = swapped(gate_low, 1)
    gate_high = halve_near(columns(gate_pair, cols, ff), z)

    def up_grads(normed_m, d_up):
        return grad_half(1, normed_m, d_up), grad_half(0, normed_m, d_up)

    up_send, up_keep = single(up_grads, normed_m, d_up)
    back_near, down_low, gate_low, gate_high, down_high, up_send, up_keep = meet(
        back_near, down_low, gate_low, gate_high, down_high, up_send, up_keep
    )
    up_got = swap_c(up_send)

    def mid_back(back_mlp, from_x, from_y, unit_m, scale_m, gain_m, cot):
        d_normed_m = scatter_sum(back_mlp, (from_x, from_y))
        d_mid = cot.astype(F32) + norm_back(d_normed_m, unit_m, gain_m, scale_m)
        return d_mid, d_mid.astype(BF), jnp.sum(d_normed_m * unit_m, axis=(0, 1))

    d_mid, d_mid_low, gain_m_part = single(mid_back, back_mlp, *back_near, unit_m, scale_m, gain_m, cot)

    d_mid_low, up_got, inner = meet(d_mid_low, up_got, inner)
    d_mid_near = gather_near(d_mid_low)
    gate_high = swapped(gate_high, 1)
    gate_low = far_steps(gate_low, z)
    gate_low = swapped(single(lambda *p: halve(p, z, far_last()), *gate_low), far)

    def mlp_out(inner, down_w):
        part = cols_cols(inner, down_w).astype(BF).reshape(micro, 4 * toks, width)
        return part, far_parts(part)

    mlp_part, mlp_far = single(mlp_out, inner, down_w)
    up_pair = up_keep, up_got
    up_halves = single(lambda *p: halve(p, z, 1), *up_pair)
    d_mid_near, d_mid_parts, gate_high, up_halves, gate_low, mlp_part = meet(
        d_mid_near, diag_parts(d_mid_near), gate_high, up_halves, gate_low, mlp_part
    )
    d_mid_diag = gather_diag(d_mid_parts)
    up_sum = swapped(up_halves, 1)
    mlp_far, d_mid_diag, gate_high, down_high = meet(mlp_far, d_mid_diag, halve_far(gate_high, z), down_high)
    d_mid_all = gather_join(d_mid_near, d_mid_diag).reshape(rows, width)
    mlp_far = scatter_far(mlp_far)
    gate_high = swapped(gate_high, far)
    down_high = swapped(down_high, far)

    def attention_back(d_mid_all, out_w, queries, keys_values, attended, cos, sin, allowed):
        d_att = jnp.dot(d_mid_all, out_w, preferred_element_type=F32).astype(BF)
        d_qkv = attend_back(queries, keys_values, d_att, cos, sin, allowed)
        return d_qkv, grad_half(1, d_mid_all, attended), grad_half(0, d_mid_all, attended)

    d_qkv, out_send, out_keep = single(
        attention_back, d_mid_all, out_w, queries, keys_values, attended, cos, sin, allowed
    )
    d_qkv, out_send, mlp_far, gate_high, up_sum, down_high = meet(
        d_qkv, out_send, mlp_far, gate_high, up_sum, down_high
    )
    out_got = swap_c(out_send)
    up_sum, ready = meet(up_sum, scatter_prep(mlp_part, mlp_far))
    mlp_near = scatter_near(*ready)
    d_qkv, up_halves = meet(d_qkv, halve_far(up_sum, z))
    up_sum = swapped(up_halves, far)
    d_qkv, out_halves = meet(d_qkv, halve_near((out_keep, out_got), z))
    out_sum = swapped(out_halves, 1)
    down_parts = reduce_y(side_by_side(down_low, down_high), y)

    def qkv_back(d_qkv, qkv_w, hid_all, scale_a, gain_m_part, normed_a):
        back = cols_cols(d_qkv, qkv_w)
        unit_a = hid_all.astype(F32).reshape(rows, width) * scale_a
        gain_rows = jnp.stack([jnp.sum(back * unit_a, axis=0), gain_m_part]).reshape(2, 2, nz, 2, block)
        gain_rows = gain_rows.transpose(1, 2, 3, 0, 4)
        back = back.astype(BF).reshape(micro, 4 * toks, width)
        grads = grad_half(1, normed_a, d_qkv), grad_half(0, normed_a, d_qkv)
        return back, far_parts(back), gain_rows[1], gain_rows[0], *grads

    back_attn, attn_far, gain_send, gain_keep, qkv_send, qkv_keep = single(
        qkv_back, d_qkv, qkv_w, hid_all, scale_a, gain_m_part, normed_a
    )
    back_attn, attn_far, qkv_send, gain_send, mlp_near, out_sum, up_sum, down_parts, gate_sum = meet(
        back_attn,
        attn_far,
        qkv_send,
        gain_send,
        mlp_near,
        out_sum,
        up_sum,
        down_parts,
        side_by_side(gate_low, gate_high),
    )
    attn_far = scatter_far(attn_far)
    gain_got = swap_c(gain_send)
    qkv_got = swap_c(qkv_send)

    qkv_got, gain_got, out_sum = meet(qkv_got, gain_got, out_sum)

    def tail_halves(qkv_pair, gain_pair, out_pair):
        return halve(qkv_pair, z, 1), halve(gain_pair, z, 1), halve(out_pair, z, far_last())

    qkv_halves, gain_halves, out_halves = single(
        tail_halves, (qkv_keep, qkv_got), (gain_keep, gain_got), far_steps(out_sum, z)
    )
    attn_far, qkv_halves, gain_halves, out_halves = meet(attn_far, qkv_halves, gain_halves, out_halves)
    qkv_sum, gain_sum = swapped(qkv_halves, 1), swapped(gain_halves, 1)
    ready, mlp_near = meet(scatter_prep(back_attn, attn_far), mlp_near)
    attn_near = scatter_near(*ready)
    out_sum = swapped(out_halves, far)

    def finish_out(mid, mlp_part, mlp_near):
        return (mid + scatter_sum(mlp_part, mlp_near)).astype(BF)

    block_out = regroup(single(finish_out, mid, mlp_part, mlp_near), block, c, True)
    qkv_sum, gain_sum, block_out = meet(qkv_sum, gain_sum, block_out)

    def far_halves(*pairs):
        return [halve(p, z, far_last()) for p in pairs]

    qkv_halves, gain_halves = single(far_halves, far_steps(qkv_sum, z), far_steps(gain_sum, z))
    attn_near, qkv_halves, gain_halves, out_sum = meet(attn_near, qkv_halves, gain_halves, out_sum)
    qkv_sum, gain_sum = swapped(qkv_halves, far), swapped(gain_halves, far)
    up_parts = reduce_y(up_sum, y)
    gate_parts = reduce_y(gate_sum, y)
    out_parts = reduce_y(out_sum, y)

    def finish_grad(back_attn, from_x, from_y, hid, scale_a, gain_a, d_mid):
        sc_a = scale_a.reshape(micro, 4 * toks, 1)[:, :toks]
        d_normed_a = scatter_sum(back_attn, (from_x, from_y))
        return d_mid + norm_back(d_normed_a, hid.astype(F32) * sc_a, gain_a, sc_a)

    input_grad = single(finish_grad, back_attn, *attn_near, hid, scale_a, gain_a, d_mid)
    input_grad = regroup(input_grad, block, c, True)
    input_grad, qkv_sum, gain_sum, up_parts, gate_parts, out_parts = meet(
        input_grad, qkv_sum, gain_sum, up_parts, gate_parts, out_parts
    )
    gain_keep, gain_send = (add(*(pick(p[0], 0, at) for p in gain_sum)) for at in (y, 1 - y))
    gain_parts = swap_x(gain_keep), swap_y(gain_send), swap_diagonal(gain_send)
    qkv_parts = reduce_y(qkv_sum, y)
    keep = gain_keep + gain_parts[0] + (gain_parts[1] + gain_parts[2])

    def cut(parts, lo, hi):
        return join((parts[0][:, lo:hi], parts[1][:, lo:hi]), y)

    return (
        block_out[:, None],
        input_grad[:, None],
        keep[0],
        keep[1],
        cut(qkv_parts, 0, q_cols),
        cut(qkv_parts, q_cols, q_cols + kv_cols),
        cut(qkv_parts, q_cols + kv_cols, qkv_cols),
        join(out_parts, y),
        join(gate_parts, y),
        join(up_parts, y),
        join(down_parts, y),
    )


def solution(mesh):
    n_dp, n_tensor = mesh.shape["dp"], mesh.shape["tensor"]
    grid = Mesh(mesh.devices.reshape(n_dp // 4, 2, 2, n_tensor), ("z", "y", "c", "x"))
    dp = ("z", "y", "c")
    token = P(None, dp, "x", None)
    weight = P(dp, "x")
    gain = P(dp)
    in_specs = (token, P(None, dp, None), gain, gain) + (weight,) * 7 + (token,)
    out_specs = (token, token, gain, gain) + (weight,) * 7
    return jax.shard_map(
        on_device, mesh=grid, in_specs=in_specs, out_specs=out_specs, check_vma=False
    )
```
